512 devices in a mesh: period: 16 (over z, core), block: 32 (over y, x).
Axes of the slice: x: 4, y: 8, z: 8, core: 2. Of those that a mesh axis runs over, the one named last changes fastest.
Arguments:
- link_rows: bfloat16 [1048576, 512], P(('period', 'block')), may hold values from -1.5 to 1.5
- barrier_weights: float32 [1048576], P(('period', 'block')), may hold values from 0.1 to 10
- row_residual: float32 [1048576], P(('period', 'block')), may hold values from -6 to 6
- tile_pattern: int32 [8192, 4], P(('period', 'block')), may hold values 0 or 1
- block_rows: int32 [512], P(('period', 'block')), may hold values from 1 to 2048, 349525 in all
- link_diag: float32 [512], replicated, may hold values from 0.05 to 0.5
Outputs:
- row_step: float32 [1048576], P(('period', 'block'))
- link_step: float32 [512], replicated
The draws below stay inside these ranges and needn't reach their ends.
Inputs may be any that keep to these rules, and one draw needn't show every extreme that they name: `block_rows`: each block has between 1 and 2048 live rows; some block has exactly 2048.
All inputs are finite; a program needn't handle non-finite values. No bound on the sum of `tile_pattern` on one device may be relied on, other than what follows from the above.
Results may differ from the reference program's by a relative error of at most 0.0055.
The reference program's roundings to bfloat16 on the way (of `masked`, `scaled`, `weighted` and `step_b`) count: a program that leaves them out, or rounds other values in their place, can miss the bound.
Values sent between devices are 32-bit elements; how exact they have to be, the bound alone decides.
No kernel may reach another device: no remote copies, remote signals or barrier semaphores. Data moves between devices by JAX's collectives and lax.ppermute only.
A program may use at most 64 MiB of HBM per device.

```python
import math
import jax
import jax.numpy as jnp
import numpy as np
from jax import lax

LINK = 512
TILE = 128
ROWS_DEV = 2048
DEVICES_ALL = 512
ROWS_TOTAL = 1048576
N_PERIOD = 16
N_BLOCK = 32


def draw_link_rows(key, part):
    chosen_key = jax.random.fold_in(key, 11)
    value_key = jax.random.fold_in(key, 12)
    chosen = jax.random.randint(chosen_key, (ROWS_TOTAL, 1), 0, ROWS_TOTAL)
    strong = chosen < 4 * LINK
    weak_scale = 0.6 / math.sqrt(ROWS_TOTAL)
    values = jnp.clip(jax.random.normal(value_key, (ROWS_TOTAL, LINK), jnp.float32), -4.0, 4.0)
    strong_values = values * 0.375
    result = jnp.where(strong, strong_values, values * weak_scale)
    row_place = lax.broadcasted_iota(jnp.int32, (ROWS_TOTAL, LINK), 0)
    column_place = lax.broadcasted_iota(jnp.int32, (ROWS_TOTAL, LINK), 1)
    owner = row_place // ROWS_DEV
    leading = row_place % ROWS_DEV == 0
    home = column_place == owner % LINK
    signed = jnp.where(values >= 0.0, jnp.float32(1.5), jnp.float32(-1.5))
    result = jnp.where(leading & home, signed, result)
    return result.astype(jnp.bfloat16)


def set_ends(values, own_key, low, largest):
    place = [jax.random.randint(jax.random.fold_in(own_key, axis), (), 0, length) for axis, length in enumerate(values.shape)]
    widest = values.shape.index(max(values.shape))
    next_to = place[:widest] + [(place[widest] + 1) % values.shape[widest]] + place[widest + 1:]
    return values.at[tuple(place)].set(low).at[tuple(next_to)].set(largest)


def level_of(own_key, extent, shards, smallest, high):
    gain, own = 1.0, jax.random.fold_in(own_key, 6)
    for axis_at, parts in shards:
        draws = jnp.exp(jax.random.uniform(jax.random.fold_in(own, axis_at), (parts,), jnp.float32, smallest / len(shards), high / len(shards)))
        gain = gain * jnp.repeat(draws, extent[axis_at] // parts).reshape([-1 if axis == axis_at else 1 for axis in range(len(extent))])
    return gain


def profile(amount, total, limit, slope):
    weights = [(1 << 20) // math.isqrt(grade ** slope) + 1 for grade in range(2, amount + 1)]
    surplus, holding = total - limit - (amount - 1), [1] * (amount - 1)
    while surplus > 0:
        free = [i for i in range(amount - 1) if holding[i] < limit]
        mass, budget = sum([weights[i] for i in free]), surplus
        for i in free:
            addition = min(limit - holding[i], max(1, budget * weights[i] // mass), surplus)
            holding[i] = holding[i] + addition
            surplus = surplus - addition
    return np.array([limit] + holding)


def uneven_parts(rng, amount, total, reach, slope):
    if amount == 2:
        one = jax.random.randint(rng, (), max(1, total - reach), min(reach, total - 1) + 1)
        return jnp.stack([one, total - one])
    sizes = jnp.asarray(profile(amount, total, reach, slope), jnp.int32)
    pairs = (amount - 1) // 2
    giver, taker = sizes[1:1 + 2 * pairs:2], sizes[2:2 + 2 * pairs:2]
    margin = jnp.minimum(giver - 1, reach - taker)
    shifted = jax.random.randint(jax.random.fold_in(rng, 1), (pairs,), 0, 1 << 20) % (margin + 1)
    sizes = sizes.at[1:1 + 2 * pairs:2].set(giver - shifted).at[2:2 + 2 * pairs:2].set(taker + shifted)
    return sizes[jax.random.permutation(jax.random.fold_in(rng, 2), amount)]


def centred(key, extent, width, limit, pieces=(), dtype=jnp.bfloat16):
    drawn = width * jax.random.normal(key, extent, jnp.float32)
    if pieces:
        drawn = drawn * level_of(key, extent, pieces, -0.22, 0.18)
    return jnp.clip(drawn, -limit, limit).astype(dtype)


def setup_inputs(seed: int = 0) -> dict:
    key_of = jax.random.split(jax.random.key(seed), 7)
    return {
        "link_rows": draw_link_rows(jax.random.fold_in(key_of[6], 71), 0),
        "barrier_weights": jnp.clip(jnp.exp(math.log(10.0) - 4.6051702 * jax.random.uniform(key_of[1], (ROWS_TOTAL,), jnp.float32) ** level_of(key_of[1], (ROWS_TOTAL,), ((0, 512),), -0.2, 0.2)), 0.1, 10.0),
        "row_residual": centred(key_of[2], (ROWS_TOTAL,), 1.0, 6.0, ((0, 512),), jnp.float32),
        "tile_pattern": set_ends((jax.random.randint(key_of[3], (ROWS_TOTAL // TILE, LINK // TILE), 0, 4) < 3).astype(jnp.int32), jax.random.fold_in(key_of[3], 1), 0, 1),
        "block_rows": uneven_parts(key_of[4], DEVICES_ALL, DEVICES_ALL * ROWS_DEV // 3, ROWS_DEV, 2).astype(jnp.int32),
        "link_diag": jnp.clip(jnp.exp(jax.random.uniform(key_of[5], (LINK,), jnp.float32, math.log(0.05), math.log(0.5))), 0.05, 0.5),
    }


def block_terms(rows, weights, resid, pattern, count):
    live = (jnp.arange(ROWS_DEV) < count).astype(jnp.float32)
    cover = jnp.repeat(jnp.repeat(pattern, TILE, axis=0), TILE, axis=1).astype(jnp.float32)
    masked = rows * (cover * live[:, None]).astype(jnp.bfloat16)
    scaled = (masked.astype(jnp.float32) * jnp.sqrt(weights)[:, None]).astype(jnp.bfloat16)
    weighted = (weights * resid * live).astype(jnp.bfloat16)
    contrib = lax.dot_general(scaled.astype(jnp.float32), scaled.astype(jnp.float32), (((0,), (0,)), ((), ())), preferred_element_type=jnp.float32)
    partial_value = lax.dot_general(masked.astype(jnp.float32), weighted.astype(jnp.float32), (((0,), (0,)), ((), ())), preferred_element_type=jnp.float32)
    return (masked, live, contrib, partial_value)

def reference(link_rows, barrier_weights, row_residual, tile_pattern, block_rows, link_diag):
    count_all = N_PERIOD * N_BLOCK
    rows_all = link_rows.reshape(count_all, ROWS_DEV, LINK)
    weights_all = barrier_weights.reshape(count_all, ROWS_DEV)
    resid_all = row_residual.reshape(count_all, ROWS_DEV)
    pattern_all = tile_pattern.reshape(count_all, ROWS_DEV // TILE, LINK // TILE)

    def accumulate(carry, items):
        rows, weights, resid, pattern, count = items
        masked, live, contrib, partial_value = block_terms(rows, weights, resid, pattern, count)
        return ((carry[0] + contrib, carry[1] + partial_value), None)
    start = (jnp.zeros((LINK, LINK), jnp.float32), jnp.zeros((LINK,), jnp.float32))
    (schur, gradient), unused = lax.scan(accumulate, start, (rows_all, weights_all, resid_all, pattern_all, block_rows))
    schur = schur + jnp.diag(link_diag)
    factor = jnp.linalg.cholesky(schur)
    link_step = jax.scipy.linalg.cho_solve((factor, True), gradient)
    step_b = link_step.astype(jnp.bfloat16)

    def row_pass(carry, items):
        rows, weights, resid, pattern, count = items
        masked, live, contrib, partial_value = block_terms(rows, weights, resid, pattern, count)
        moved = jnp.dot(masked.astype(jnp.float32), step_b.astype(jnp.float32), preferred_element_type=jnp.float32)
        return (carry, live * weights * (moved - resid))
    unused, row_step = lax.scan(row_pass, jnp.float32(0.0), (rows_all, weights_all, resid_all, pattern_all, block_rows))
    return (row_step.reshape(ROWS_TOTAL), link_step)
```

```python
import functools

import jax
import jax.numpy as jnp
from jax import lax
from jax.experimental import pallas as pl
from jax.experimental.pallas import tpu as pltpu
from jax.sharding import Mesh, PartitionSpec as P

TILE = 128
WIDTH = 512
ROWS = 2048
TILES = ROWS // TILE
CHUNKS = 4
F32 = jnp.float32
BF16 = jnp.bfloat16
HIGH = lax.Precision.HIGHEST
HALF = 544
NAMES = ("z", "core", "y", "x")


def iota(shape, axis):
    return lax.broadcasted_iota(jnp.int32, shape, axis)


def dot_nn(a, b):
    return lax.dot_general(a, b, (((1,), (0,)), ((), ())), precision=HIGH, preferred_element_type=F32)


def dot_nt(a, b):
    return lax.dot_general(a, b, (((1,), (1,)), ((), ())), precision=HIGH, preferred_element_type=F32)


def assemble_kernel(count_ref, pattern_ref, rows_hbm, weights_ref, resid_ref, out_ref, rows, scaled, sems):
    step = ROWS // CHUNKS
    copies = [
        pltpu.make_async_copy(rows_hbm.at[pl.ds(i * step, step)], rows.at[pl.ds(i * step, step)], sems.at[i])
        for i in range(CHUNKS)
    ]
    for copy in copies:
        copy.start()
    count = count_ref[0]
    shape = (TILES, TILE)
    live = (iota(shape, 0) * TILE + iota(shape, 1) < count).astype(F32)
    weights = weights_ref[...]
    root = jnp.sqrt(weights) * live
    weighted = (weights * resid_ref[...] * live).astype(BF16).astype(F32)
    columns = jnp.concatenate([root, weighted, jnp.zeros((TILE - 2 * TILES, TILE), F32)], axis=0).T
    gradient = [jnp.zeros((8, TILE), F32) for _ in range(4)]
    for t in range(TILES):
        if t % (TILES // CHUNKS) == 0:
            copies[t // (TILES // CHUNKS)].wait()
        root_t = jnp.broadcast_to(columns[:, t : t + 1], (TILE, TILE))
        weighted_t = jnp.broadcast_to(columns[:, TILES + t : TILES + t + 1], (TILE, TILE))
        for j in range(4):
            cover = pattern_ref[t, j].astype(F32)
            x = rows[pl.ds(t * TILE, TILE), pl.ds(j * TILE, TILE)].astype(F32) * cover
            scaled[pl.ds(t * TILE, TILE), pl.ds(j * TILE, TILE)] = (x * root_t).astype(BF16)
            gradient[j] = gradient[j] + jnp.sum((x * weighted_t).reshape(TILE // 8, 8, TILE), axis=0)
    below = iota((TILE, TILE), 0) >= iota((TILE, TILE), 1)
    same = iota((TILE, TILE), 0) == iota((TILE, TILE), 1)

    def gram(i, j):
        return lax.dot_general(
            scaled[:, pl.ds(i * 256, 256)],
            scaled[:, pl.ds(j * 256, 256)],
            (((0,), (0,)), ((), ())),
            preferred_element_type=F32,
        )

    def finish(base, block, corner, pieces, first):
        a, b = block[:TILE, :TILE], block[TILE:, TILE:]
        out_ref[pl.ds(base, TILE), :] = jnp.where(below, a, b)
        out_ref[pl.ds(base + TILE, TILE), :] = corner
        for i, piece in enumerate(pieces):
            out_ref[pl.ds(base + (2 + i) * TILE, TILE), :] = piece
        diagonal = jnp.sum(jnp.where(same, b, 0.0), axis=0, keepdims=True)
        parts = [jnp.sum(gradient[first], axis=0, keepdims=True), jnp.sum(gradient[first + 1], axis=0, keepdims=True), diagonal]
        out_ref[pl.ds(base + 4 * TILE, 8), :] = jnp.concatenate(parts + [jnp.zeros((5, TILE), F32)], axis=0)
        out_ref[pl.ds(base + 4 * TILE + 8, 24), :] = jnp.zeros((24, TILE), F32)

    top, low, cross = gram(0, 0), gram(1, 1), gram(1, 0)
    finish(0, top, top[TILE:, :TILE], (cross[:TILE, :TILE], cross[TILE:, :TILE]), 0)
    finish(HALF, low, low[TILE:, :TILE], (cross[:TILE, TILE:], cross[TILE:, TILE:]), 2)


def assemble(count, pattern, rows, weights, resid):
    vmem = pl.BlockSpec(memory_space=pltpu.VMEM)
    smem = pl.BlockSpec(memory_space=pltpu.SMEM)
    return pl.pallas_call(
        assemble_kernel,
        out_shape=jax.ShapeDtypeStruct((2 * HALF, TILE), F32),
        in_specs=[smem, smem, pl.BlockSpec(memory_space=pl.ANY), vmem, vmem],
        out_specs=vmem,
        scratch_shapes=[
            pltpu.VMEM((ROWS, WIDTH), BF16),
            pltpu.VMEM((ROWS, WIDTH), BF16),
            pltpu.SemaphoreType.DMA((CHUNKS,)),
        ],
        name="assemble",
    )(count, pattern, rows, weights, resid)


def invert(block):
    groups = [block[8 * i : 8 * i + 8, :] for i in range(16)]
    lane, sub = iota((8, TILE), 1), iota((8, TILE), 0)
    wide = lambda v: jnp.broadcast_to(v, (8, TILE))
    for k in range(16):
        split = [[wide(g[:, 8 * k + j : 8 * k + j + 1]) for j in range(8)] for g in groups]
        inside = (lane >= 8 * k) & (lane < 8 * k + 8)
        panel = jnp.where(inside, (lane - 8 * k == sub).astype(F32), groups[k])
        cols = list(split[k])
        for j in range(8):
            here = sub == j
            inverse = 1.0 / wide(cols[j][j : j + 1, :])
            pivot = cols[j]
            scaled_row = wide(panel[j : j + 1, :]) * inverse
            panel = jnp.where(here, scaled_row, panel - pivot * scaled_row)
            for c in range(j + 1, 8):
                entry = wide(cols[c][j : j + 1, :]) * inverse
                cols[c] = jnp.where(here, entry, cols[c] - pivot * entry)
        spread = [wide(panel[j : j + 1, :]) for j in range(8)]
        for i in range(16):
            if i != k:
                terms = [split[i][j] * spread[j] for j in range(8)]
                total = ((terms[0] + terms[1]) + (terms[2] + terms[3])) + ((terms[4] + terms[5]) + (terms[6] + terms[7]))
                groups[i] = jnp.where(inside, 0.0, groups[i]) - total
        groups[k] = panel
    return jnp.concatenate(groups, axis=0)


def solve_kernel(
    count_ref, rows_hbm, packed_ref, diag_ref, weights_ref, resid_ref, pattern_ref, row_step_ref, step_ref,
    rows, matrix, inverses, sem,
):
    copy = pltpu.make_async_copy(rows_hbm, rows, sem)
    copy.start()
    below = iota((TILE, TILE), 0) >= iota((TILE, TILE), 1)
    same = iota((TILE, TILE), 0) == iota((TILE, TILE), 1)
    link = diag_ref[...]

    def tile(i, j):
        return pl.ds(i * TILE, TILE), pl.ds(j * TILE, TILE)

    gradient = []
    for h in range(2):
        base = h * HALF
        folded = packed_ref[pl.ds(base, TILE), :]
        turned = folded.T
        extras = packed_ref[pl.ds(base + 4 * TILE, 8), :]
        gradient += [extras[0:1], extras[1:2]]
        i = 2 * h
        matrix[tile(i, i)] = jnp.where(below, folded, turned) + jnp.where(same, link[i : i + 1, :], 0.0)
        matrix[tile(i + 1, i + 1)] = jnp.where(same, extras[2:3] + link[i + 1 : i + 2, :], jnp.where(below, turned, folded))
        matrix[tile(i + 1, i)] = packed_ref[pl.ds(base + TILE, TILE), :]
        matrix[tile(2, h)] = packed_ref[pl.ds(base + 2 * TILE, TILE), :]
        matrix[tile(3, h)] = packed_ref[pl.ds(base + 3 * TILE, TILE), :]
    factors = {}
    for k in range(4):
        inverse = invert(matrix[tile(k, k)])
        inverses[k] = inverse
        for i in range(k + 1, 4):
            factors[i, k] = dot_nn(matrix[tile(i, k)], inverse)
        for i in range(k + 1, 4):
            gradient[i] = gradient[i] - dot_nt(gradient[k], factors[i, k])
            for j in range(k + 1, i + 1):
                matrix[tile(i, j)] = matrix[tile(i, j)] - dot_nt(factors[i, k], matrix[tile(j, k)])
    steps = [None] * 4
    for k in reversed(range(4)):
        value = dot_nn(gradient[k], inverses[k])
        for i in range(k + 1, 4):
            value = value - dot_nn(steps[i], factors[i, k])
        steps[k] = value
    step_ref[...] = jnp.concatenate(steps, axis=0)
    copy.wait()
    rounded = [jnp.broadcast_to(v, (TILES, TILE)) for v in steps]
    present = pattern_ref[...].astype(F32)
    left = jnp.concatenate(
        [v * jnp.broadcast_to(present[:, j : j + 1], (TILES, TILE)) for j, v in enumerate(rounded)], axis=1
    ).astype(BF16)
    shape = (TILES, TILE)
    moved = jnp.zeros(shape, F32)
    for t in range(TILES):
        part = lax.dot_general(
            left, rows[pl.ds(t * TILE, TILE), :], (((1,), (1,)), ((), ())), preferred_element_type=F32
        )
        moved = jnp.where(iota(shape, 0) == t, part, moved)
    live = (iota(shape, 0) * TILE + iota(shape, 1) < count_ref[0]).astype(F32)
    row_step_ref[...] = live * weights_ref[...] * (moved - resid_ref[...])


def solve(count, rows, packed, diag, weights, resid, pattern):
    vmem = pl.BlockSpec(memory_space=pltpu.VMEM)
    smem = pl.BlockSpec(memory_space=pltpu.SMEM)
    return pl.pallas_call(
        solve_kernel,
        out_shape=(jax.ShapeDtypeStruct((TILES, TILE), F32), jax.ShapeDtypeStruct((4, TILE), F32)),
        in_specs=[smem, pl.BlockSpec(memory_space=pl.ANY), vmem, vmem, vmem, vmem, vmem],
        out_specs=(vmem, vmem),
        scratch_shapes=[
            pltpu.VMEM((ROWS, WIDTH), BF16),
            pltpu.VMEM((WIDTH, WIDTH), F32),
            pltpu.VMEM((4, TILE, TILE), F32),
            pltpu.SemaphoreType.DMA,
        ],
        name="solve",
    )(count, rows, packed, diag, weights, resid, pattern)


def exchange(x, axes):
    return lax.all_to_all(x, axes, split_axis=0, concat_axis=0, tiled=True)


def reduce_all(packed):
    core = lax.axis_index("core")
    keep = lax.dynamic_slice_in_dim(packed, core * HALF, HALF, 0)
    give = lax.dynamic_slice_in_dim(packed, (1 - core) * HALF, HALF, 0)
    swap = [(0, 1), (1, 0)]
    half = keep + lax.ppermute(give, "core", swap)
    pieces = exchange(half.reshape(32, 17, TILE), ("y", "x"))
    piece = jnp.sum(pieces, axis=0)
    layers = exchange(jnp.broadcast_to(piece[None], (8, 17, TILE)), "z")
    piece = jnp.sum(layers, axis=0)
    half = exchange(jnp.broadcast_to(piece[None], (32, 17, TILE)), ("y", "x")).reshape(HALF, TILE)
    other = lax.ppermute(half, "core", swap)
    return jnp.where(core == 0, jnp.concatenate([half, other]), jnp.concatenate([other, half]))


def on_device(link_rows, barrier_weights, row_residual, tile_pattern, block_rows, link_diag):
    weights = barrier_weights.reshape(TILES, TILE)
    resid = row_residual.reshape(TILES, TILE)
    packed = assemble(block_rows, tile_pattern, link_rows, weights, resid)
    packed = reduce_all(packed)
    row_step, step = solve(block_rows, link_rows, packed, link_diag.reshape(4, TILE), weights, resid, tile_pattern)
    return row_step.reshape(ROWS), step.reshape(WIDTH)


def solution(mesh):
    fine = Mesh(mesh.devices.reshape(8, 2, 8, 4), NAMES)
    return jax.shard_map(
        on_device,
        mesh=fine,
        in_specs=(P(NAMES, None), P(NAMES), P(NAMES), P(NAMES, None), P(NAMES), P()),
        out_specs=(P(NAMES), P()),
        check_vma=False,
    )
```

```python
import functools

import jax
import jax.numpy as jnp
from jax import lax
from jax.experimental import pallas as pl
from jax.experimental.pallas import tpu as pltpu
from jax.sharding import Mesh, PartitionSpec as P

TILE = 128
WIDTH = 512
ROWS = 2048
TILES = ROWS // TILE
CHUNKS = 4
F32 = jnp.float32
BF16 = jnp.bfloat16
HIGH = lax.Precision.HIGHEST
HALF = 544
NAMES = ("z", "core", "y", "x")


def iota(shape, axis):
    return lax.broadcasted_iota(jnp.int32, shape, axis)


def dot_nn(a, b):
    return lax.dot_general(a, b, (((1,), (0,)), ((), ())), precision=HIGH, preferred_element_type=F32)


def dot_nt(a, b):
    return lax.dot_general(a, b, (((1,), (1,)), ((), ())), precision=HIGH, preferred_element_type=F32)


def assemble_kernel(
    core_ref, count_ref, pattern_ref, rows_hbm, weights_ref, resid_ref, keep_ref, give_ref, rows, scaled, sems
):
    step = ROWS // CHUNKS
    copies = [
        pltpu.make_async_copy(rows_hbm.at[pl.ds(i * step, step)], rows.at[pl.ds(i * step, step)], sems.at[i])
        for i in range(CHUNKS)
    ]
    for copy in copies:
        copy.start()
    count = count_ref[0]
    shape = (TILES, TILE)
    live = (iota(shape, 0) * TILE + iota(shape, 1) < count).astype(F32)
    weights = weights_ref[...]
    root = jnp.sqrt(weights) * live
    weighted = (weights * resid_ref[...] * live).astype(BF16).astype(F32)
    columns = jnp.concatenate([root, weighted, jnp.zeros((TILE - 2 * TILES, TILE), F32)], axis=0).T
    gradient = [jnp.zeros((8, TILE), F32) for _ in range(4)]
    for t in range(TILES):
        if t % (TILES // CHUNKS) == 0:
            copies[t // (TILES // CHUNKS)].wait()
        root_t = jnp.broadcast_to(columns[:, t : t + 1], (TILE, TILE))
        weighted_t = jnp.broadcast_to(columns[:, TILES + t : TILES + t + 1], (TILE, TILE))
        for j in range(4):
            cover = pattern_ref[j, t].astype(F32)
            x = rows[pl.ds(t * TILE, TILE), pl.ds(j * TILE, TILE)].astype(F32) * cover
            scaled[pl.ds(t * TILE, TILE), pl.ds(j * TILE, TILE)] = (x * root_t).astype(BF16)
            gradient[j] = gradient[j] + jnp.sum((x * weighted_t).reshape(TILE // 8, 8, TILE), axis=0)
    below = iota((TILE, TILE), 0) >= iota((TILE, TILE), 1)
    same = iota((TILE, TILE), 0) == iota((TILE, TILE), 1)

    def gram(i, j):
        return lax.dot_general(
            scaled[:, pl.ds(i * 256, 256)],
            scaled[:, pl.ds(j * 256, 256)],
            (((0,), (0,)), ((), ())),
            preferred_element_type=F32,
        )

    def finish(out_ref, block, corner, pieces, first):
        a, b = block[:TILE, :TILE], block[TILE:, TILE:]
        out_ref[pl.ds(0, TILE), :] = jnp.where(below, a, b)
        out_ref[pl.ds(TILE, TILE), :] = corner
        for i, piece in enumerate(pieces):
            out_ref[pl.ds((2 + i) * TILE, TILE), :] = piece
        diagonal = jnp.sum(jnp.where(same, b, 0.0), axis=0, keepdims=True)
        parts = [jnp.sum(gradient[first], axis=0, keepdims=True), jnp.sum(gradient[first + 1], axis=0, keepdims=True), diagonal]
        out_ref[pl.ds(4 * TILE, 8), :] = jnp.concatenate(parts + [jnp.zeros((5, TILE), F32)], axis=0)
        out_ref[pl.ds(4 * TILE + 8, 24), :] = jnp.zeros((24, TILE), F32)

    top, low, cross = gram(0, 0), gram(1, 1), gram(1, 0)

    def both(first_ref, second_ref):
        finish(first_ref, top, top[TILE:, :TILE], (cross[:TILE, :TILE], cross[TILE:, :TILE]), 0)
        finish(second_ref, low, low[TILE:, :TILE], (cross[:TILE, TILE:], cross[TILE:, TILE:]), 2)

    @pl.when(core_ref[0] == 0)
    def _():
        both(keep_ref, give_ref)

    @pl.when(core_ref[0] != 0)
    def _():
        both(give_ref, keep_ref)


def assemble(core, count, pattern, rows, weights, resid):
    vmem = pl.BlockSpec(memory_space=pltpu.VMEM)
    smem = pl.BlockSpec(memory_space=pltpu.SMEM)
    half = jax.ShapeDtypeStruct((HALF, TILE), F32)
    return pl.pallas_call(
        assemble_kernel,
        out_shape=(half, half),
        in_specs=[smem, smem, smem, pl.BlockSpec(memory_space=pl.ANY), vmem, vmem],
        out_specs=(vmem, vmem),
        scratch_shapes=[
            pltpu.VMEM((ROWS, WIDTH), BF16),
            pltpu.VMEM((ROWS, WIDTH), BF16),
            pltpu.SemaphoreType.DMA((CHUNKS,)),
        ],
        name="assemble",
    )(core, count, pattern, rows, weights, resid)


def wide(v):
    return jnp.broadcast_to(v, (8, TILE))


def eliminate(groups, first):
    lane, sub = iota((8, TILE), 1), iota((8, TILE), 0)
    groups = list(groups)
    for k in range(8):
        start = first + 8 * k
        cols = [wide(groups[k][:, start + j : start + j + 1]) for j in range(8)]
        inside = (lane >= start) & (lane < start + 8)
        panel = jnp.where(inside, (lane - start == sub).astype(F32), groups[k])
        for j in range(8):
            here = sub == j
            inverse = 1.0 / wide(cols[j][j : j + 1, :])
            pivot = cols[j]
            scaled_row = wide(panel[j : j + 1, :]) * inverse
            panel = jnp.where(here, scaled_row, panel - pivot * scaled_row)
            for c in range(j + 1, 8):
                entry = wide(cols[c][j : j + 1, :]) * inverse
                cols[c] = jnp.where(here, entry, cols[c] - pivot * entry)
        spread = [wide(panel[j : j + 1, :]) for j in range(8)]
        order = [(k + 1 + i) % 8 for i in range(7)]
        for i in order:
            terms = [wide(groups[i][:, start + j : start + j + 1]) * spread[j] for j in range(8)]
            total = ((terms[0] + terms[1]) + (terms[2] + terms[3])) + ((terms[4] + terms[5]) + (terms[6] + terms[7]))
            groups[i] = jnp.where(inside, 0.0, groups[i]) - total
        groups[k] = panel
    return groups


def invert(block):
    half = TILE // 2
    lane = iota((half, TILE), 1)
    zeros = jnp.zeros((half, TILE), F32)
    top, low = block[:half], block[half:]
    split = lambda v: [v[8 * i : 8 * i + 8] for i in range(8)]
    top = jnp.concatenate(eliminate(split(top), 0), axis=0)
    low = jnp.where(lane < half, 0.0, low) - dot_nn(low, jnp.concatenate([top, zeros], axis=0))
    low = jnp.concatenate(eliminate(split(low), half), axis=0)
    top = jnp.where(lane < half, top, 0.0) - dot_nn(top, jnp.concatenate([zeros, low], axis=0))
    return jnp.concatenate([top, low], axis=0)


def solve_kernel(
    core_ref, count_ref, pattern_ref, rows_hbm, mine_ref, other_ref, diag_ref, weights_ref, resid_ref,
    row_step_ref, step_ref, rows, matrix, inverses, sem,
):
    copy = pltpu.make_async_copy(rows_hbm, rows, sem)
    copy.start()
    below = iota((TILE, TILE), 0) >= iota((TILE, TILE), 1)
    same = iota((TILE, TILE), 0) == iota((TILE, TILE), 1)
    link = diag_ref[...]
    core = core_ref[0]

    def tile(i, j):
        return pl.ds(i * TILE, TILE), pl.ds(j * TILE, TILE)

    gradient = []
    for h in range(2):

        def part(start, size):
            return jnp.where(core == h, mine_ref[pl.ds(start, size), :], other_ref[pl.ds(start, size), :])

        folded = part(0, TILE)
        turned = folded.T
        extras = part(4 * TILE, 8)
        gradient += [extras[0:1], extras[1:2]]
        i = 2 * h
        matrix[tile(i, i)] = jnp.where(below, folded, turned) + jnp.where(same, link[i : i + 1, :], 0.0)
        matrix[tile(i + 1, i + 1)] = jnp.where(same, extras[2:3] + link[i + 1 : i + 2, :], jnp.where(below, turned, folded))
        matrix[tile(i + 1, i)] = part(TILE, TILE)
        matrix[tile(2, h)] = part(2 * TILE, TILE)
        matrix[tile(3, h)] = part(3 * TILE, TILE)
    factors = {}
    for k in range(4):
        inverse = invert(matrix[tile(k, k)])
        inverses[k] = inverse
        for i in range(k + 1, 4):
            factors[i, k] = dot_nn(matrix[tile(i, k)], inverse)
        for i in range(k + 1, 4):
            gradient[i] = gradient[i] - dot_nt(gradient[k], factors[i, k])
            for j in range(k + 1, i + 1):
                matrix[tile(i, j)] = matrix[tile(i, j)] - dot_nt(factors[i, k], matrix[tile(j, k)])
    steps = [None] * 4
    for k in reversed(range(4)):
        value = dot_nn(gradient[k], inverses[k])
        for i in range(k + 1, 4):
            value = value - dot_nn(steps[i], factors[i, k])
        steps[k] = value
    step_ref[...] = jnp.concatenate(steps, axis=0)
    copy.wait()
    shape = (TILES, TILE)
    left = []
    for j in range(4):
        present = jnp.zeros(shape, F32)
        for t in range(TILES):
            present = jnp.where(iota(shape, 0) == t, pattern_ref[j, t].astype(F32), present)
        left.append(jnp.broadcast_to(steps[j], shape) * present)
    left = jnp.concatenate(left, axis=1).astype(BF16)
    moved = jnp.zeros(shape, F32)
    for t in range(TILES):
        part = lax.dot_general(
            left, rows[pl.ds(t * TILE, TILE), :], (((1,), (1,)), ((), ())), preferred_element_type=F32
        )
        moved = jnp.where(iota(shape, 0) == t, part, moved)
    live = (iota(shape, 0) * TILE + iota(shape, 1) < count_ref[0]).astype(F32)
    row_step_ref[...] = live * weights_ref[...] * (moved - resid_ref[...])


def solve(core, count, pattern, rows, mine, other, diag, weights, resid):
    vmem = pl.BlockSpec(memory_space=pltpu.VMEM)
    smem = pl.BlockSpec(memory_space=pltpu.SMEM)
    return pl.pallas_call(
        solve_kernel,
        out_shape=(jax.ShapeDtypeStruct((TILES, TILE), F32), jax.ShapeDtypeStruct((4, TILE), F32)),
        in_specs=[smem, smem, smem, pl.BlockSpec(memory_space=pl.ANY)] + [vmem] * 5,
        out_specs=(vmem, vmem),
        scratch_shapes=[
            pltpu.VMEM((ROWS, WIDTH), BF16),
            pltpu.VMEM((WIDTH, WIDTH), F32),
            pltpu.VMEM((4, TILE, TILE), F32),
            pltpu.SemaphoreType.DMA,
        ],
        name="solve",
    )(core, count, pattern, rows, mine, other, diag, weights, resid)


def exchange(x, axes):
    return lax.all_to_all(x, axes, split_axis=0, concat_axis=0, tiled=True)


def reduce_all(keep, give):
    swap = [(0, 1), (1, 0)]
    half = keep + lax.ppermute(give, "core", swap)
    pieces = exchange(half.reshape(32, 17, TILE), ("y", "x"))
    piece = jnp.sum(pieces, axis=0)
    layers = exchange(jnp.broadcast_to(piece[None], (8, 17, TILE)), "z")
    piece = jnp.sum(layers, axis=0)
    half = exchange(jnp.broadcast_to(piece[None], (32, 17, TILE)), ("y", "x")).reshape(HALF, TILE)
    return half, lax.ppermute(half, "core", swap)


def on_device(link_rows, barrier_weights, row_residual, tile_pattern, block_rows, link_diag):
    weights = barrier_weights.reshape(TILES, TILE)
    resid = row_residual.reshape(TILES, TILE)
    core = lax.axis_index("core").astype(jnp.int32).reshape(1)
    pattern = tile_pattern.T
    mine, other = reduce_all(*assemble(core, block_rows, pattern, link_rows, weights, resid))
    row_step, step = solve(core, block_rows, pattern, link_rows, mine, other, link_diag.reshape(4, TILE), weights, resid)
    return row_step.reshape(ROWS), step.reshape(WIDTH)


def solution(mesh):
    fine = Mesh(mesh.devices.reshape(8, 2, 8, 4), NAMES)
    return jax.shard_map(
        on_device,
        mesh=fine,
        in_specs=(P(NAMES, None), P(NAMES), P(NAMES), P(NAMES, None), P(NAMES), P()),
        out_specs=(P(NAMES), P()),
        check_vma=False,
    )
```

```python
import functools

import jax
import jax.numpy as jnp
from jax import lax
from jax.experimental import pallas as pl
from jax.experimental.pallas import tpu as pltpu
from jax.sharding import Mesh, PartitionSpec as P

TILE = 128
WIDTH = 512
ROWS = 2048
TILES = ROWS // TILE
CHUNKS = 4
F32 = jnp.float32
BF16 = jnp.bfloat16
HIGH = lax.Precision.HIGHEST
HALF = 544
NAMES = ("z", "core", "y", "x")


def iota(shape, axis):
    return lax.broadcasted_iota(jnp.int32, shape, axis)


def dot_nn(a, b):
    return lax.dot_general(a, b, (((1,), (0,)), ((), ())), precision=HIGH, preferred_element_type=F32)


def dot_nt(a, b):
    return lax.dot_general(a, b, (((1,), (1,)), ((), ())), precision=HIGH, preferred_element_type=F32)


def assemble_kernel(
    core_ref, count_ref, pattern_ref, rows_hbm, weights_ref, resid_ref, keep_ref, give_ref, rows, scaled, sems
):
    step = ROWS // CHUNKS
    copies = [
        pltpu.make_async_copy(rows_hbm.at[pl.ds(i * step, step)], rows.at[pl.ds(i * step, step)], sems.at[i])
        for i in range(CHUNKS)
    ]
    for copy in copies:
        copy.start()
    count = count_ref[0]
    shape = (TILES, TILE)
    live = (iota(shape, 0) * TILE + iota(shape, 1) < count).astype(F32)
    weights = weights_ref[...]
    root = jnp.sqrt(weights) * live
    weighted = (weights * resid_ref[...] * live).astype(BF16).astype(F32)
    columns = jnp.concatenate([root, weighted, jnp.zeros((TILE - 2 * TILES, TILE), F32)], axis=0).T
    gradient = [jnp.zeros((8, TILE), F32) for _ in range(4)]
    for t in range(TILES):
        if t % (TILES // CHUNKS) == 0:
            copies[t // (TILES // CHUNKS)].wait()
        root_t = jnp.broadcast_to(columns[:, t : t + 1], (TILE, TILE))
        weighted_t = jnp.broadcast_to(columns[:, TILES + t : TILES + t + 1], (TILE, TILE))
        for j in range(4):
            cover = pattern_ref[j, t].astype(F32)
            x = rows[pl.ds(t * TILE, TILE), pl.ds(j * TILE, TILE)].astype(F32) * cover
            scaled[pl.ds(t * TILE, TILE), pl.ds(j * TILE, TILE)] = (x * root_t).astype(BF16)
            gradient[j] = gradient[j] + jnp.sum((x * weighted_t).reshape(TILE // 8, 8, TILE), axis=0)
    below = iota((TILE, TILE), 0) >= iota((TILE, TILE), 1)
    same = iota((TILE, TILE), 0) == iota((TILE, TILE), 1)

    def gram(i, j):
        return lax.dot_general(
            scaled[:, pl.ds(i * 256, 256)],
            scaled[:, pl.ds(j * 256, 256)],
            (((0,), (0,)), ((), ())),
            preferred_element_type=F32,
        )

    def finish(out_ref, block, corner, pieces, first):
        a, b = block[:TILE, :TILE], block[TILE:, TILE:]
        out_ref[pl.ds(0, TILE), :] = jnp.where(below, a, b)
        out_ref[pl.ds(TILE, TILE), :] = corner
        for i, piece in enumerate(pieces):
            out_ref[pl.ds((2 + i) * TILE, TILE), :] = piece
        diagonal = jnp.sum(jnp.where(same, b, 0.0), axis=0, keepdims=True)
        parts = [jnp.sum(gradient[first], axis=0, keepdims=True), jnp.sum(gradient[first + 1], axis=0, keepdims=True), diagonal]
        out_ref[pl.ds(4 * TILE, 8), :] = jnp.concatenate(parts + [jnp.zeros((5, TILE), F32)], axis=0)
        out_ref[pl.ds(4 * TILE + 8, 24), :] = jnp.zeros((24, TILE), F32)

    top, low, cross = gram(0, 0), gram(1, 1), gram(1, 0)

    def both(first_ref, second_ref):
        finish(first_ref, top, top[TILE:, :TILE], (cross[:TILE, :TILE], cross[TILE:, :TILE]), 0)
        finish(second_ref, low, low[TILE:, :TILE], (cross[:TILE, TILE:], cross[TILE:, TILE:]), 2)

    @pl.when(core_ref[0] == 0)
    def _():
        both(keep_ref, give_ref)

    @pl.when(core_ref[0] != 0)
    def _():
        both(give_ref, keep_ref)


def assemble(core, count, pattern, rows, weights, resid):
    vmem = pl.BlockSpec(memory_space=pltpu.VMEM)
    smem = pl.BlockSpec(memory_space=pltpu.SMEM)
    half = jax.ShapeDtypeStruct((HALF, TILE), F32)
    return pl.pallas_call(
        assemble_kernel,
        out_shape=(half, half),
        in_specs=[smem, smem, smem, pl.BlockSpec(memory_space=pl.ANY), vmem, vmem],
        out_specs=(vmem, vmem),
        scratch_shapes=[
            pltpu.VMEM((ROWS, WIDTH), BF16),
            pltpu.VMEM((ROWS, WIDTH), BF16),
            pltpu.SemaphoreType.DMA((CHUNKS,)),
        ],
        name="assemble",
    )(core, count, pattern, rows, weights, resid)


def wide(v):
    return jnp.broadcast_to(v, (8, TILE))


def spread_lane(v, lane):
    return jnp.take_along_axis(v, jnp.full((8, TILE), lane, jnp.int32), axis=1)


def eliminate(rows, first, once, tasks):
    lane, sub = iota((8, TILE), 1), iota((8, TILE), 0)
    groups = [rows[8 * k : 8 * k + 8] for k in range(8)]
    sides = [(lane - first - 8 * k == sub).astype(F32) for k in range(8)]
    lower, scaled = [], []
    for k in range(8):
        start = first + 8 * k

        todo = tasks.pop(0) if tasks and k >= tasks[0][0] else None

        def body(_, carry):
            if todo:
                todo[1]()
            groups, sides = list(carry[: 8 - k]), list(carry[8 - k :])
            cols = [spread_lane(groups[0], start + j) for j in range(8)]
            panel, side = groups[0], sides[0]
            for j in range(8):
                here = sub == j
                pivot = cols[j]
                inverse = 1.0 / wide(pivot[j : j + 1, :])
                row, side_row = wide(panel[j : j + 1, :]) * inverse, wide(side[j : j + 1, :]) * inverse
                for c in range(j + 1, 8):
                    entry = wide(cols[c][j : j + 1, :]) * inverse
                    cols[c] = jnp.where(here, entry, cols[c] - pivot * entry)
                panel = jnp.where(here, row, panel - pivot * row)
                side = jnp.where(here, side_row, side - pivot * side_row)
            spread = [wide(panel[j : j + 1, :]) for j in range(8)]
            spread_side = [wide(side[j : j + 1, :]) for j in range(8)]
            for i in range(1, 8 - k):
                lead = [spread_lane(groups[i], start + j) for j in range(8)]
                groups[i] = groups[i] - add_up([lead[j] * spread[j] for j in range(8)])
                sides[i] = sides[i] - add_up([lead[j] * spread_side[j] for j in range(8)])
            return (*groups[1:], panel, *sides[1:], side)

        lower.append(sides[0])
        carry = lax.fori_loop(0, once, body, (*groups, *sides))
        groups, sides = list(carry[: 7 - k]), list(carry[8 - k : -1])
        scaled.append(carry[-1])
    return jnp.concatenate(lower, axis=0), jnp.concatenate(scaled, axis=0)


def add_up(terms):
    while len(terms) > 1:
        terms = [terms[i] + terms[i + 1] for i in range(0, len(terms), 2)]
    return terms[0]


def thirds(x):
    high = x.astype(BF16)
    rest = x - high.astype(F32)
    middle = rest.astype(BF16)
    return high, middle, (rest - middle.astype(F32)).astype(BF16)


def as_left(x):
    h, m, l = thirds(x)
    return jnp.concatenate([h, m, h, m, h, l], axis=1)


def as_right(x, axis=1):
    h, m, l = thirds(x)
    return jnp.concatenate([h, h, m, m, l, h], axis=axis)


def times(left, right, dim=1):
    return lax.dot_general(left, right, (((1,), (dim,)), ((), ())), preferred_element_type=F32)


def factor(block, once, cross, tasks):
    half = TILE // 2
    zeros = jnp.zeros((half, TILE), F32)
    low = block[half:]
    lower, scaled = eliminate(block[:half], 0, once, tasks)
    pair = times(as_left(low), as_right(jnp.concatenate([lower, zeros, scaled, zeros], axis=0)))
    left = as_left(pair[:, :TILE])
    low = low - times(left, as_right(jnp.concatenate([zeros, pair[:, TILE:]], axis=0)))
    cross[pl.ds(half, half), :] = times(left, as_right(jnp.concatenate([scaled, zeros], axis=0), 0), 0)
    both = jnp.concatenate(eliminate(low, half, once, tasks), axis=0)
    both = both - times(as_left(both), as_right(cross[...], 0), 0)
    return jnp.concatenate([lower, both[:half]], axis=0), jnp.concatenate([scaled, both[half:]], axis=0)


def solve_kernel(
    core_ref, count_ref, pattern_ref, rows_hbm, mine_ref, other_ref, diag_ref, weights_ref, resid_ref,
    row_step_ref, step_ref, rows, matrix, lefts, left_parts, right_parts, both_parts, scales, cross, sem,
):
    copy = pltpu.make_async_copy(rows_hbm, rows, sem)
    copy.start()
    below = iota((TILE, TILE), 0) >= iota((TILE, TILE), 1)
    same = iota((TILE, TILE), 0) == iota((TILE, TILE), 1)
    link = diag_ref[...]
    core = core_ref[0]

    def tile(i, j):
        return pl.ds(i * TILE, TILE), pl.ds(j * TILE, TILE)

    gradient = []
    for h in range(2):

        def part(start, size):
            return jnp.where(core == h, mine_ref[pl.ds(start, size), :], other_ref[pl.ds(start, size), :])

        folded = part(0, TILE)
        turned = folded.T
        extras = part(4 * TILE, 8)
        gradient += [extras[0:1], extras[1:2]]
        i = 2 * h
        matrix[tile(i, i)] = jnp.where(below, folded, turned) + jnp.where(same, link[i : i + 1, :], 0.0)
        matrix[tile(i + 1, i + 1)] = jnp.where(same, extras[2:3] + link[i + 1 : i + 2, :], jnp.where(below, turned, folded))
        matrix[tile(i + 1, i)] = part(TILE, TILE)
        matrix[tile(2, h)] = part(2 * TILE, TILE)
        matrix[tile(3, h)] = part(3 * TILE, TILE)
    once = jnp.minimum(count_ref[0], 1)
    cross[...] = jnp.zeros((TILE, TILE), F32)
    matrix[pl.ds(WIDTH, 16), :] = jnp.broadcast_to(jnp.concatenate(gradient, axis=1), (16, WIDTH))

    def span(i):
        return pl.ds(i * TILE, TILE if i < 3 else TILE + 16)

    def project(i, q, both):
        pair = times(as_left(matrix[span(i), pl.ds(q * TILE, TILE)]), both)
        lefts[q, span(i), :] = pair[:, :TILE]
        left_parts[span(i), :] = as_left(pair[:, :TILE])
        right_parts[pl.ds(i * TILE, TILE), :] = as_right(pair[:TILE, TILE:])

    def update(i, j, count):
        columns = pl.ds(j * TILE, count * TILE)
        matrix[span(i), columns] -= times(left_parts[span(i), :], right_parts[columns, :])

    tasks = []
    for q in range(4):
        lower, scaled = factor(matrix[tile(q, q)], once, cross, tasks)
        assert not tasks
        scales[q] = scaled
        both_parts[...] = as_right(jnp.concatenate([lower, scaled], axis=0))
        if q == 3:
            break
        project(q + 1, q, both_parts[...])
        update(q + 1, q + 1, 1)
        for i in range(q + 2, 4):
            tasks.append((1, functools.partial(lambda i, q: project(i, q, both_parts[...]), i, q)))
        for i in range(q + 2, 4):
            tasks.append((1, functools.partial(update, i, q + 1, 2)))
            if i == q + 3:
                tasks.append((1, functools.partial(update, i, i, 1)))
    last = times(as_left(matrix[pl.ds(WIDTH, 16), pl.ds(3 * TILE, TILE)]), both_parts[pl.ds(0, TILE), :])
    steps = [None] * 4
    for q in reversed(range(4)):
        value = last[:1] if q == 3 else lefts[q, pl.ds(WIDTH, 8), :][:1]
        for i in range(q + 1, 4):
            value = value - dot_nn(steps[i], lefts[q, pl.ds(i * TILE, TILE), :])
        steps[q] = dot_nn(value, scales[q])
    step_ref[...] = jnp.concatenate(steps, axis=0)
    copy.wait()
    shape = (TILES, TILE)
    left = []
    for j in range(4):
        present = jnp.zeros(shape, F32)
        for t in range(TILES):
            present = jnp.where(iota(shape, 0) == t, pattern_ref[j, t].astype(F32), present)
        left.append(jnp.broadcast_to(steps[j], shape) * present)
    left = jnp.concatenate(left, axis=1).astype(BF16)
    moved = jnp.zeros(shape, F32)
    for t in range(TILES):
        part = lax.dot_general(
            left, rows[pl.ds(t * TILE, TILE), :], (((1,), (1,)), ((), ())), preferred_element_type=F32
        )
        moved = jnp.where(iota(shape, 0) == t, part, moved)
    live = (iota(shape, 0) * TILE + iota(shape, 1) < count_ref[0]).astype(F32)
    row_step_ref[...] = live * weights_ref[...] * (moved - resid_ref[...])


def solve(core, count, pattern, rows, mine, other, diag, weights, resid):
    vmem = pl.BlockSpec(memory_space=pltpu.VMEM)
    smem = pl.BlockSpec(memory_space=pltpu.SMEM)
    return pl.pallas_call(
        solve_kernel,
        out_shape=(jax.ShapeDtypeStruct((TILES, TILE), F32), jax.ShapeDtypeStruct((4, TILE), F32)),
        in_specs=[smem, smem, smem, pl.BlockSpec(memory_space=pl.ANY)] + [vmem] * 5,
        out_specs=(vmem, vmem),
        scratch_shapes=[
            pltpu.VMEM((ROWS, WIDTH), BF16),
            pltpu.VMEM((WIDTH + 16, WIDTH), F32),
            pltpu.VMEM((3, WIDTH + 16, TILE), F32),
            pltpu.VMEM((WIDTH + 16, 6 * TILE), BF16),
            pltpu.VMEM((WIDTH, 6 * TILE), BF16),
            pltpu.VMEM((2 * TILE, 6 * TILE), BF16),
            pltpu.VMEM((4, TILE, TILE), F32),
            pltpu.VMEM((TILE, TILE), F32),
            pltpu.SemaphoreType.DMA,
        ],
        name="solve",
    )(core, count, pattern, rows, mine, other, diag, weights, resid)


def exchange(x, axes):
    return lax.all_to_all(x, axes, split_axis=0, concat_axis=0, tiled=True)


def reduce_all(keep, give):
    swap = [(0, 1), (1, 0)]
    half = keep + lax.ppermute(give, "core", swap)
    pieces = exchange(half.reshape(32, 17, TILE), ("y", "x"))
    piece = jnp.sum(pieces, axis=0)
    layers = exchange(jnp.broadcast_to(piece[None], (8, 17, TILE)), "z")
    piece = jnp.sum(layers, axis=0)
    half = exchange(jnp.broadcast_to(piece[None], (32, 17, TILE)), ("y", "x")).reshape(HALF, TILE)
    return half, lax.ppermute(half, "core", swap)


def on_device(link_rows, barrier_weights, row_residual, tile_pattern, block_rows, link_diag):
    weights = barrier_weights.reshape(TILES, TILE)
    resid = row_residual.reshape(TILES, TILE)
    core = lax.axis_index("core").astype(jnp.int32).reshape(1)
    pattern = tile_pattern.T
    mine, other = reduce_all(*assemble(core, block_rows, pattern, link_rows, weights, resid))
    row_step, step = solve(core, block_rows, pattern, link_rows, mine, other, link_diag.reshape(4, TILE), weights, resid)
    return row_step.reshape(ROWS), step.reshape(WIDTH)


def solution(mesh):
    fine = Mesh(mesh.devices.reshape(8, 2, 8, 4), NAMES)
    return jax.shard_map(
        on_device,
        mesh=fine,
        in_specs=(P(NAMES, None), P(NAMES), P(NAMES), P(NAMES, None), P(NAMES), P()),
        out_specs=(P(NAMES), P()),
        check_vma=False,
    )
```

```python
import functools

import jax
import jax.numpy as jnp
from jax import lax
from jax.experimental import pallas as pl
from jax.experimental.pallas import tpu as pltpu
from jax.sharding import Mesh, PartitionSpec as P

TILE = 128
WIDTH = 512
ROWS = 2048
TILES = ROWS // TILE
CHUNKS = 4
F32 = jnp.float32
BF16 = jnp.bfloat16
HIGH = lax.Precision.HIGHEST
HALF = 544
NAMES = ("z", "core", "y", "x")


def iota(shape, axis):
    return lax.broadcasted_iota(jnp.int32, shape, axis)


def dot_nn(a, b):
    return lax.dot_general(a, b, (((1,), (0,)), ((), ())), precision=HIGH, preferred_element_type=F32)


def dot_nt(a, b):
    return lax.dot_general(a, b, (((1,), (1,)), ((), ())), precision=HIGH, preferred_element_type=F32)


def assemble_kernel(
    core_ref, count_ref, pattern_ref, rows_hbm, weights_ref, resid_ref, keep_ref, give_ref, rows, scaled, sems
):
    step = ROWS // CHUNKS
    copies = [
        pltpu.make_async_copy(rows_hbm.at[pl.ds(i * step, step)], rows.at[pl.ds(i * step, step)], sems.at[i])
        for i in range(CHUNKS)
    ]
    for copy in copies:
        copy.start()
    count = count_ref[0]
    shape = (TILES, TILE)
    live = (iota(shape, 0) * TILE + iota(shape, 1) < count).astype(F32)
    weights = weights_ref[...]
    root = jnp.sqrt(weights) * live
    weighted = (weights * resid_ref[...] * live).astype(BF16).astype(F32)
    columns = jnp.concatenate([root, weighted, jnp.zeros((TILE - 2 * TILES, TILE), F32)], axis=0).T
    gradient = [jnp.zeros((8, TILE), F32) for _ in range(4)]
    for t in range(TILES):
        if t % (TILES // CHUNKS) == 0:
            copies[t // (TILES // CHUNKS)].wait()
        root_t = jnp.broadcast_to(columns[:, t : t + 1], (TILE, TILE))
        weighted_t = jnp.broadcast_to(columns[:, TILES + t : TILES + t + 1], (TILE, TILE))
        for j in range(4):
            cover = pattern_ref[j, t].astype(F32)
            x = rows[pl.ds(t * TILE, TILE), pl.ds(j * TILE, TILE)].astype(F32) * cover
            scaled[pl.ds(t * TILE, TILE), pl.ds(j * TILE, TILE)] = (x * root_t).astype(BF16)
            gradient[j] = gradient[j] + jnp.sum((x * weighted_t).reshape(TILE // 8, 8, TILE), axis=0)
    below = iota((TILE, TILE), 0) >= iota((TILE, TILE), 1)
    same = iota((TILE, TILE), 0) == iota((TILE, TILE), 1)

    def gram(i, j):
        return lax.dot_general(
            scaled[:, pl.ds(i * 256, 256)],
            scaled[:, pl.ds(j * 256, 256)],
            (((0,), (0,)), ((), ())),
            preferred_element_type=F32,
        )

    def finish(out_ref, block, corner, pieces, first):
        a, b = block[:TILE, :TILE], block[TILE:, TILE:]
        out_ref[pl.ds(0, TILE), :] = jnp.where(below, a, b)
        out_ref[pl.ds(TILE, TILE), :] = corner
        for i, piece in enumerate(pieces):
            out_ref[pl.ds((2 + i) * TILE, TILE), :] = piece
        diagonal = jnp.sum(jnp.where(same, b, 0.0), axis=0, keepdims=True)
        parts = [jnp.sum(gradient[first], axis=0, keepdims=True), jnp.sum(gradient[first + 1], axis=0, keepdims=True), diagonal]
        out_ref[pl.ds(4 * TILE, 8), :] = jnp.concatenate(parts + [jnp.zeros((5, TILE), F32)], axis=0)
        out_ref[pl.ds(4 * TILE + 8, 24), :] = jnp.zeros((24, TILE), F32)

    top, low, cross = gram(0, 0), gram(1, 1), gram(1, 0)

    def both(first_ref, second_ref):
        finish(first_ref, top, top[TILE:, :TILE], (cross[:TILE, :TILE], cross[TILE:, :TILE]), 0)
        finish(second_ref, low, low[TILE:, :TILE], (cross[:TILE, TILE:], cross[TILE:, TILE:]), 2)

    @pl.when(core_ref[0] == 0)
    def _():
        both(keep_ref, give_ref)

    @pl.when(core_ref[0] != 0)
    def _():
        both(give_ref, keep_ref)


def assemble(core, count, pattern, rows, weights, resid):
    vmem = pl.BlockSpec(memory_space=pltpu.VMEM)
    smem = pl.BlockSpec(memory_space=pltpu.SMEM)
    half = pltpu.VMEM((HALF, TILE), F32)
    return pl.pallas_call(
        assemble_kernel,
        out_shape=(half, half),
        in_specs=[smem, smem, smem, pl.BlockSpec(memory_space=pl.ANY), vmem, vmem],
        out_specs=(vmem, vmem),
        scratch_shapes=[
            pltpu.VMEM((ROWS, WIDTH), BF16),
            pltpu.VMEM((ROWS, WIDTH), BF16),
            pltpu.SemaphoreType.DMA((CHUNKS,)),
        ],
        name="assemble",
    )(core, count, pattern, rows, weights, resid)


def wide(v):
    return jnp.broadcast_to(v, (8, TILE))


def spread_lane(v, lane):
    return jnp.take_along_axis(v, jnp.full((8, TILE), lane, jnp.int32), axis=1)


def eliminate(rows, first, once, tasks):
    lane, sub = iota((8, TILE), 1), iota((8, TILE), 0)
    groups = [rows[8 * k : 8 * k + 8] for k in range(8)]
    sides = [(lane - first - 8 * k == sub).astype(F32) for k in range(8)]
    lower, scaled = [], []
    for k in range(8):
        start = first + 8 * k

        todo = tasks.pop(0) if tasks and k >= tasks[0][0] else None

        def body(_, carry):
            if todo:
                todo[1]()
            groups, sides = list(carry[: 8 - k]), list(carry[8 - k :])
            cols = [spread_lane(groups[0], start + j) for j in range(8)]
            panel, side = groups[0], sides[0]
            for j in range(8):
                here = sub == j
                pivot = cols[j]
                inverse = 1.0 / wide(pivot[j : j + 1, :])
                row, side_row = wide(panel[j : j + 1, :]) * inverse, wide(side[j : j + 1, :]) * inverse
                for c in range(j + 1, 8):
                    entry = wide(cols[c][j : j + 1, :]) * inverse
                    cols[c] = jnp.where(here, entry, cols[c] - pivot * entry)
                panel = jnp.where(here, row, panel - pivot * row)
                side = jnp.where(here, side_row, side - pivot * side_row)
            spread = [wide(panel[j : j + 1, :]) for j in range(8)]
            spread_side = [wide(side[j : j + 1, :]) for j in range(8)]
            for i in range(1, 8 - k):
                lead = [spread_lane(groups[i], start + j) for j in range(8)]
                groups[i] = groups[i] - add_up([lead[j] * spread[j] for j in range(8)])
                sides[i] = sides[i] - add_up([lead[j] * spread_side[j] for j in range(8)])
            return (*groups[1:], panel, *sides[1:], side)

        lower.append(sides[0])
        carry = lax.fori_loop(0, once, body, (*groups, *sides))
        groups, sides = list(carry[: 7 - k]), list(carry[8 - k : -1])
        scaled.append(carry[-1])
    return jnp.concatenate(lower, axis=0), jnp.concatenate(scaled, axis=0)


def add_up(terms):
    while len(terms) > 1:
        terms = [terms[i] + terms[i + 1] for i in range(0, len(terms), 2)]
    return terms[0]


def thirds(x):
    high = x.astype(BF16)
    rest = x - high.astype(F32)
    middle = rest.astype(BF16)
    return high, middle, (rest - middle.astype(F32)).astype(BF16)


def as_left(x):
    h, m, l = thirds(x)
    return jnp.concatenate([h, m, h, m, h, l], axis=1)


def as_right(x, axis=1):
    h, m, l = thirds(x)
    return jnp.concatenate([h, h, m, m, l, h], axis=axis)


def times(left, right, dim=1):
    return lax.dot_general(left, right, (((1,), (dim,)), ((), ())), preferred_element_type=F32)


def factor(block, once, cross, tasks):
    half = TILE // 2
    zeros = jnp.zeros((half, TILE), F32)
    low = block[half:]
    lower, scaled = eliminate(block[:half], 0, once, tasks)
    pair = times(as_left(low), as_right(jnp.concatenate([lower, zeros, scaled, zeros], axis=0)))
    left = as_left(pair[:, :TILE])
    low = low - times(left, as_right(jnp.concatenate([zeros, pair[:, TILE:]], axis=0)))
    cross[pl.ds(half, half), :] = times(left, as_right(jnp.concatenate([scaled, zeros], axis=0), 0), 0)
    both = jnp.concatenate(eliminate(low, half, once, tasks), axis=0)
    both = both - times(as_left(both), as_right(cross[...], 0), 0)
    return jnp.concatenate([lower, both[:half]], axis=0), jnp.concatenate([scaled, both[half:]], axis=0)


def solve_kernel(
    core_ref, count_ref, pattern_ref, rows_hbm, mine_ref, other_ref, diag_ref, weights_ref, resid_ref,
    row_step_ref, step_ref, rows, matrix, lefts, left_parts, right_parts, both_parts, scales, cross, sem,
):
    copy = pltpu.make_async_copy(rows_hbm, rows, sem)
    copy.start()
    below = iota((TILE, TILE), 0) >= iota((TILE, TILE), 1)
    same = iota((TILE, TILE), 0) == iota((TILE, TILE), 1)
    link = diag_ref[...]
    core = core_ref[0]

    def tile(i, j):
        return pl.ds(i * TILE, TILE), pl.ds(j * TILE, TILE)

    gradient = []
    for h in range(2):

        def part(start, size):
            return jnp.where(core == h, mine_ref[pl.ds(start, size), :], other_ref[pl.ds(start, size), :])

        folded = part(0, TILE)
        turned = folded.T
        extras = part(4 * TILE, 8)
        gradient += [extras[0:1], extras[1:2]]
        i = 2 * h
        matrix[tile(i, i)] = jnp.where(below, folded, turned) + jnp.where(same, link[i : i + 1, :], 0.0)
        matrix[tile(i + 1, i + 1)] = jnp.where(same, extras[2:3] + link[i + 1 : i + 2, :], jnp.where(below, turned, folded))
        matrix[tile(i + 1, i)] = part(TILE, TILE)
        matrix[tile(2, h)] = part(2 * TILE, TILE)
        matrix[tile(3, h)] = part(3 * TILE, TILE)
    once = jnp.minimum(count_ref[0], 1)
    cross[...] = jnp.zeros((TILE, TILE), F32)
    matrix[pl.ds(WIDTH, 16), :] = jnp.broadcast_to(jnp.concatenate(gradient, axis=1), (16, WIDTH))

    def span(i):
        return pl.ds(i * TILE, TILE if i < 3 else TILE + 16)

    def project(i, q, both):
        pair = times(as_left(matrix[span(i), pl.ds(q * TILE, TILE)]), both)
        lefts[q, span(i), :] = pair[:, :TILE]
        left_parts[span(i), :] = as_left(pair[:, :TILE])
        right_parts[pl.ds(i * TILE, TILE), :] = as_right(pair[:TILE, TILE:])

    def update(i, j, count):
        columns = pl.ds(j * TILE, count * TILE)
        matrix[span(i), columns] -= times(left_parts[span(i), :], right_parts[columns, :])

    tasks = []
    for q in range(4):
        lower, scaled = factor(matrix[tile(q, q)], once, cross, tasks)
        assert not tasks
        scales[q] = scaled
        both_parts[...] = as_right(jnp.concatenate([lower, scaled], axis=0))
        if q == 3:
            break
        project(q + 1, q, both_parts[...])
        update(q + 1, q + 1, 1)
        for i in range(q + 2, 4):
            tasks.append((1, functools.partial(lambda i, q: project(i, q, both_parts[...]), i, q)))
        for i in range(q + 2, 4):
            tasks.append((1, functools.partial(update, i, q + 1, 2)))
            if i == q + 3:
                tasks.append((1, functools.partial(update, i, i, 1)))
    last = times(as_left(matrix[pl.ds(WIDTH, 16), pl.ds(3 * TILE, TILE)]), both_parts[pl.ds(0, TILE), :])
    steps = [None] * 4
    for q in reversed(range(4)):
        value = last[:1] if q == 3 else lefts[q, pl.ds(WIDTH, 8), :][:1]
        for i in range(q + 1, 4):
            value = value - dot_nn(steps[i], lefts[q, pl.ds(i * TILE, TILE), :])
        steps[q] = dot_nn(value, scales[q])
    step_ref[...] = jnp.concatenate(steps, axis=0)
    copy.wait()
    shape = (TILES, TILE)
    left = []
    for j in range(4):
        present = jnp.zeros(shape, F32)
        for t in range(TILES):
            present = jnp.where(iota(shape, 0) == t, pattern_ref[j, t].astype(F32), present)
        left.append(jnp.broadcast_to(steps[j], shape) * present)
    left = jnp.concatenate(left, axis=1).astype(BF16)
    moved = jnp.zeros(shape, F32)
    for t in range(TILES):
        part = lax.dot_general(
            left, rows[pl.ds(t * TILE, TILE), :], (((1,), (1,)), ((), ())), preferred_element_type=F32
        )
        moved = jnp.where(iota(shape, 0) == t, part, moved)
    live = (iota(shape, 0) * TILE + iota(shape, 1) < count_ref[0]).astype(F32)
    row_step_ref[...] = live * weights_ref[...] * (moved - resid_ref[...])


def solve(core, count, pattern, rows, mine, other, diag, weights, resid):
    vmem = pl.BlockSpec(memory_space=pltpu.VMEM)
    smem = pl.BlockSpec(memory_space=pltpu.SMEM)
    return pl.pallas_call(
        solve_kernel,
        out_shape=(jax.ShapeDtypeStruct((TILES, TILE), F32), jax.ShapeDtypeStruct((4, TILE), F32)),
        in_specs=[smem, smem, smem, pl.BlockSpec(memory_space=pl.ANY)] + [vmem] * 5,
        out_specs=(vmem, vmem),
        scratch_shapes=[
            pltpu.VMEM((ROWS, WIDTH), BF16),
            pltpu.VMEM((WIDTH + 16, WIDTH), F32),
            pltpu.VMEM((3, WIDTH + 16, TILE), F32),
            pltpu.VMEM((WIDTH + 16, 6 * TILE), BF16),
            pltpu.VMEM((WIDTH, 6 * TILE), BF16),
            pltpu.VMEM((2 * TILE, 6 * TILE), BF16),
            pltpu.VMEM((4, TILE, TILE), F32),
            pltpu.VMEM((TILE, TILE), F32),
            pltpu.SemaphoreType.DMA,
        ],
        name="solve",
    )(core, count, pattern, rows, mine, other, diag, weights, resid)


def exchange(x, axes):
    return lax.all_to_all(x, axes, split_axis=0, concat_axis=0, tiled=True)


def reduce_all(keep, give):
    swap = [(0, 1), (1, 0)]
    half = keep + lax.ppermute(give, "core", swap)
    pieces = exchange(half.reshape(32, 17, TILE), ("y", "x"))
    piece = jnp.sum(pieces, axis=0)
    layers = exchange(jnp.broadcast_to(piece[None], (8, 17, TILE)), "z")
    piece = jnp.sum(layers, axis=0)
    half = exchange(jnp.broadcast_to(piece[None], (32, 17, TILE)), ("y", "x")).reshape(HALF, TILE)
    return half, lax.ppermute(half, "core", swap)


def on_device(link_rows, barrier_weights, row_residual, tile_pattern, block_rows, link_diag):
    weights = barrier_weights.reshape(TILES, TILE)
    resid = row_residual.reshape(TILES, TILE)
    core = lax.axis_index("core").astype(jnp.int32).reshape(1)
    pattern = tile_pattern.T
    mine, other = reduce_all(*assemble(core, block_rows, pattern, link_rows, weights, resid))
    mine = pltpu.with_memory_space_constraint(mine, pltpu.VMEM)
    other = pltpu.with_memory_space_constraint(other, pltpu.VMEM)
    row_step, step = solve(core, block_rows, pattern, link_rows, mine, other, link_diag.reshape(4, TILE), weights, resid)
    return row_step.reshape(ROWS), step.reshape(WIDTH)


def solution(mesh):
    fine = Mesh(mesh.devices.reshape(8, 2, 8, 4), NAMES)
    return jax.shard_map(
        on_device,
        mesh=fine,
        in_specs=(P(NAMES, None), P(NAMES), P(NAMES), P(NAMES, None), P(NAMES), P()),
        out_specs=(P(NAMES), P()),
        check_vma=False,
    )
```

```python
import functools

import jax
import jax.numpy as jnp
from jax import lax
from jax.experimental import pallas as pl
from jax.experimental.pallas import tpu as pltpu
from jax.sharding import Mesh, PartitionSpec as P

TILE = 128
WIDTH = 512
ROWS = 2048
TILES = ROWS // TILE
CHUNKS = 4
F32 = jnp.float32
BF16 = jnp.bfloat16
HIGH = lax.Precision.HIGHEST
HALF = 544
NAMES = ("z", "core", "y", "x")


def iota(shape, axis):
    return lax.broadcasted_iota(jnp.int32, shape, axis)


def dot_nn(a, b):
    return lax.dot_general(a, b, (((1,), (0,)), ((), ())), precision=HIGH, preferred_element_type=F32)


def dot_nt(a, b):
    return lax.dot_general(a, b, (((1,), (1,)), ((), ())), precision=HIGH, preferred_element_type=F32)


def assemble_kernel(
    core_ref, count_ref, pattern_ref, rows_hbm, weights_ref, resid_ref, keep_ref, give_ref, rows, scaled, sems
):
    step = ROWS // CHUNKS
    copies = [
        pltpu.make_async_copy(rows_hbm.at[pl.ds(i * step, step)], rows.at[pl.ds(i * step, step)], sems.at[i])
        for i in range(CHUNKS)
    ]
    for copy in copies:
        copy.start()
    count = count_ref[0]
    shape = (TILES, TILE)
    live = (iota(shape, 0) * TILE + iota(shape, 1) < count).astype(F32)
    weights = weights_ref[...]
    root = jnp.sqrt(weights) * live
    weighted = (weights * resid_ref[...] * live).astype(BF16).astype(F32)
    columns = jnp.concatenate([root, weighted, jnp.zeros((TILE - 2 * TILES, TILE), F32)], axis=0).T
    gradient = [jnp.zeros((8, TILE), F32) for _ in range(4)]
    for t in range(TILES):
        if t % (TILES // CHUNKS) == 0:
            copies[t // (TILES // CHUNKS)].wait()
        root_t = jnp.broadcast_to(columns[:, t : t + 1], (TILE, TILE))
        weighted_t = jnp.broadcast_to(columns[:, TILES + t : TILES + t + 1], (TILE, TILE))
        for j in range(4):
            cover = pattern_ref[j, t].astype(F32)
            x = rows[pl.ds(t * TILE, TILE), pl.ds(j * TILE, TILE)].astype(F32) * cover
            scaled[pl.ds(t * TILE, TILE), pl.ds(j * TILE, TILE)] = (x * root_t).astype(BF16)
            gradient[j] = gradient[j] + jnp.sum((x * weighted_t).reshape(TILE // 8, 8, TILE), axis=0)
    below = iota((TILE, TILE), 0) >= iota((TILE, TILE), 1)
    same = iota((TILE, TILE), 0) == iota((TILE, TILE), 1)

    def gram(i, j):
        return lax.dot_general(
            scaled[:, pl.ds(i * 256, 256)],
            scaled[:, pl.ds(j * 256, 256)],
            (((0,), (0,)), ((), ())),
            preferred_element_type=F32,
        )

    def finish(out_ref, block, corner, pieces, first):
        a, b = block[:TILE, :TILE], block[TILE:, TILE:]
        out_ref[pl.ds(0, TILE), :] = jnp.where(below, a, b)
        out_ref[pl.ds(TILE, TILE), :] = corner
        for i, piece in enumerate(pieces):
            out_ref[pl.ds((2 + i) * TILE, TILE), :] = piece
        diagonal = jnp.sum(jnp.where(same, b, 0.0), axis=0, keepdims=True)
        parts = [jnp.sum(gradient[first], axis=0, keepdims=True), jnp.sum(gradient[first + 1], axis=0, keepdims=True), diagonal]
        out_ref[pl.ds(4 * TILE, 8), :] = jnp.concatenate(parts + [jnp.zeros((5, TILE), F32)], axis=0)
        out_ref[pl.ds(4 * TILE + 8, 24), :] = jnp.zeros((24, TILE), F32)

    top, low, cross = gram(0, 0), gram(1, 1), gram(1, 0)

    def both(first_ref, second_ref):
        finish(first_ref, top, top[TILE:, :TILE], (cross[:TILE, :TILE], cross[TILE:, :TILE]), 0)
        finish(second_ref, low, low[TILE:, :TILE], (cross[:TILE, TILE:], cross[TILE:, TILE:]), 2)

    @pl.when(core_ref[0] == 0)
    def _():
        both(keep_ref, give_ref)

    @pl.when(core_ref[0] != 0)
    def _():
        both(give_ref, keep_ref)


def assemble(core, count, pattern, rows, weights, resid):
    vmem = pl.BlockSpec(memory_space=pltpu.VMEM)
    smem = pl.BlockSpec(memory_space=pltpu.SMEM)
    half = pltpu.VMEM((HALF, TILE), F32)
    return pl.pallas_call(
        assemble_kernel,
        out_shape=(half, half),
        in_specs=[smem, smem, smem, pl.BlockSpec(memory_space=pl.ANY), vmem, vmem],
        out_specs=(vmem, vmem),
        scratch_shapes=[
            pltpu.VMEM((ROWS, WIDTH), BF16),
            pltpu.VMEM((ROWS, WIDTH), BF16),
            pltpu.SemaphoreType.DMA((CHUNKS,)),
        ],
        name="assemble",
    )(core, count, pattern, rows, weights, resid)


def wide(v):
    return jnp.broadcast_to(v, (8, TILE))


def spread_lane(v, lane):
    return jnp.take_along_axis(v, jnp.full((8, TILE), lane, jnp.int32), axis=1)


def eliminate(rows, first, once, tasks):
    lane, sub = iota((8, TILE), 1), iota((8, TILE), 0)
    groups = [rows[8 * k : 8 * k + 8] for k in range(8)]
    sides = [(lane - first - 8 * k == sub).astype(F32) for k in range(8)]
    lower, scaled = [], []
    for k in range(8):
        start = first + 8 * k

        todo = tasks.pop(0) if tasks and k >= tasks[0][0] else None

        def body(_, carry):
            if todo:
                todo[1]()
            groups, sides = list(carry[: 8 - k]), list(carry[8 - k :])
            cols = [spread_lane(groups[0], start + j) for j in range(8)]
            panel, side = groups[0], sides[0]
            for j in range(0, 8, 2):
                one, two = cols[j], cols[j + 1]
                a, b, c = wide(one[j : j + 1, :]), wide(two[j : j + 1, :]), wide(two[j + 1 : j + 2, :])
                inverse = 1.0 / (a * c - b * b)
                upper, lower_row = sub == j, sub == j + 1
                both = upper | lower_row
                by_first = jnp.where(upper, -c, jnp.where(lower_row, b, one * c - two * b)) * inverse
                by_second = jnp.where(upper, b, jnp.where(lower_row, -a, two * a - one * b)) * inverse

                def pivot(v):
                    x, y = wide(v[j : j + 1, :]), wide(v[j + 1 : j + 2, :])
                    return jnp.where(both, 0.0, v) - (by_first * x + by_second * y)

                for i in range(j + 2, 8):
                    cols[i] = pivot(cols[i])
                panel, side = pivot(panel), pivot(side)
            spread = [wide(panel[j : j + 1, :]) for j in range(8)]
            spread_side = [wide(side[j : j + 1, :]) for j in range(8)]
            for i in range(1, 8 - k):
                lead = [spread_lane(groups[i], start + j) for j in range(8)]
                groups[i] = groups[i] - add_up([lead[j] * spread[j] for j in range(8)])
                sides[i] = sides[i] - add_up([lead[j] * spread_side[j] for j in range(8)])
            return (*groups[1:], panel, *sides[1:], side)

        lower.append(sides[0])
        carry = lax.fori_loop(0, once, body, (*groups, *sides))
        groups, sides = list(carry[: 7 - k]), list(carry[8 - k : -1])
        scaled.append(carry[-1])
    return jnp.concatenate(lower, axis=0), jnp.concatenate(scaled, axis=0)


def add_up(terms):
    while len(terms) > 1:
        terms = [terms[i] + terms[i + 1] for i in range(0, len(terms), 2)]
    return terms[0]


def thirds(x):
    high = x.astype(BF16)
    rest = x - high.astype(F32)
    middle = rest.astype(BF16)
    return high, middle, (rest - middle.astype(F32)).astype(BF16)


def as_left(x):
    h, m, l = thirds(x)
    return jnp.concatenate([h, m, h, m, h, l], axis=1)


def as_right(x, axis=1):
    h, m, l = thirds(x)
    return jnp.concatenate([h, h, m, m, l, h], axis=axis)


def times(left, right, dim=1):
    return lax.dot_general(left, right, (((1,), (dim,)), ((), ())), preferred_element_type=F32)


def factor(block, once, cross, tasks):
    half = TILE // 2
    zeros = jnp.zeros((half, TILE), F32)
    low = block[half:]
    lower, scaled = eliminate(block[:half], 0, once, tasks)
    pair = times(as_left(low), as_right(jnp.concatenate([lower, zeros, scaled, zeros], axis=0)))
    left = as_left(pair[:, :TILE])
    low = low - times(left, as_right(jnp.concatenate([zeros, pair[:, TILE:]], axis=0)))
    cross[pl.ds(half, half), :] = times(left, as_right(jnp.concatenate([scaled, zeros], axis=0), 0), 0)
    both = jnp.concatenate(eliminate(low, half, once, tasks), axis=0)
    both = both - times(as_left(both), as_right(cross[...], 0), 0)
    return jnp.concatenate([lower, both[:half]], axis=0), jnp.concatenate([scaled, both[half:]], axis=0)


def solve_kernel(
    core_ref, count_ref, pattern_ref, rows_hbm, mine_ref, other_ref, diag_ref, weights_ref, resid_ref,
    row_step_ref, step_ref, rows, matrix, lefts, left_parts, right_parts, both_parts, scales, cross, sem,
):
    copy = pltpu.make_async_copy(rows_hbm, rows, sem)
    copy.start()
    below = iota((TILE, TILE), 0) >= iota((TILE, TILE), 1)
    same = iota((TILE, TILE), 0) == iota((TILE, TILE), 1)
    link = diag_ref[...]
    core = core_ref[0]

    def tile(i, j):
        return pl.ds(i * TILE, TILE), pl.ds(j * TILE, TILE)

    gradient = []
    for h in range(2):

        def part(start, size):
            return jnp.where(core == h, mine_ref[pl.ds(start, size), :], other_ref[pl.ds(start, size), :])

        folded = part(0, TILE)
        turned = folded.T
        extras = part(4 * TILE, 8)
        gradient += [extras[0:1], extras[1:2]]
        i = 2 * h
        matrix[tile(i, i)] = jnp.where(below, folded, turned) + jnp.where(same, link[i : i + 1, :], 0.0)
        matrix[tile(i + 1, i + 1)] = jnp.where(same, extras[2:3] + link[i + 1 : i + 2, :], jnp.where(below, turned, folded))
        matrix[tile(i + 1, i)] = part(TILE, TILE)
        matrix[tile(2, h)] = part(2 * TILE, TILE)
        matrix[tile(3, h)] = part(3 * TILE, TILE)
    once = jnp.minimum(count_ref[0], 1)
    cross[...] = jnp.zeros((TILE, TILE), F32)
    matrix[pl.ds(WIDTH, 16), :] = jnp.broadcast_to(jnp.concatenate(gradient, axis=1), (16, WIDTH))

    def span(i):
        return pl.ds(i * TILE, TILE if i < 3 else TILE + 16)

    def project(i, q, both):
        pair = times(as_left(matrix[span(i), pl.ds(q * TILE, TILE)]), both)
        lefts[q, span(i), :] = pair[:, :TILE]
        left_parts[span(i), :] = as_left(pair[:, :TILE])
        right_parts[pl.ds(i * TILE, TILE), :] = as_right(pair[:TILE, TILE:])

    def update(i, j, count):
        columns = pl.ds(j * TILE, count * TILE)
        matrix[span(i), columns] -= times(left_parts[span(i), :], right_parts[columns, :])

    tasks = []
    for q in range(4):
        lower, scaled = factor(matrix[tile(q, q)], once, cross, tasks)
        assert not tasks
        scales[q] = scaled
        both_parts[...] = as_right(jnp.concatenate([lower, scaled], axis=0))
        if q == 3:
            break
        project(q + 1, q, both_parts[...])
        update(q + 1, q + 1, 1)
        for i in range(q + 2, 4):
            tasks.append((1, functools.partial(lambda i, q: project(i, q, both_parts[...]), i, q)))
        for i in range(q + 2, 4):
            tasks.append((1, functools.partial(update, i, q + 1, 2)))
            if i == q + 3:
                tasks.append((1, functools.partial(update, i, i, 1)))
    last = times(as_left(matrix[pl.ds(WIDTH, 16), pl.ds(3 * TILE, TILE)]), both_parts[pl.ds(0, TILE), :])
    steps = [None] * 4
    for q in reversed(range(4)):
        value = last[:1] if q == 3 else lefts[q, pl.ds(WIDTH, 8), :][:1]
        for i in range(q + 1, 4):
            value = value - dot_nn(steps[i], lefts[q, pl.ds(i * TILE, TILE), :])
        steps[q] = dot_nn(value, scales[q])
    step_ref[...] = jnp.concatenate(steps, axis=0)
    copy.wait()
    shape = (TILES, TILE)
    left = []
    for j in range(4):
        present = jnp.zeros(shape, F32)
        for t in range(TILES):
            present = jnp.where(iota(shape, 0) == t, pattern_ref[j, t].astype(F32), present)
        left.append(jnp.broadcast_to(steps[j], shape) * present)
    left = jnp.concatenate(left, axis=1).astype(BF16)
    moved = jnp.zeros(shape, F32)
    for t in range(TILES):
        part = lax.dot_general(
            left, rows[pl.ds(t * TILE, TILE), :], (((1,), (1,)), ((), ())), preferred_element_type=F32
        )
        moved = jnp.where(iota(shape, 0) == t, part, moved)
    live = (iota(shape, 0) * TILE + iota(shape, 1) < count_ref[0]).astype(F32)
    row_step_ref[...] = live * weights_ref[...] * (moved - resid_ref[...])


def solve(core, count, pattern, rows, mine, other, diag, weights, resid):
    vmem = pl.BlockSpec(memory_space=pltpu.VMEM)
    smem = pl.BlockSpec(memory_space=pltpu.SMEM)
    return pl.pallas_call(
        solve_kernel,
        out_shape=(jax.ShapeDtypeStruct((TILES, TILE), F32), jax.ShapeDtypeStruct((4, TILE), F32)),
        in_specs=[smem, smem, smem, pl.BlockSpec(memory_space=pl.ANY)] + [vmem] * 5,
        out_specs=(vmem, vmem),
        scratch_shapes=[
            pltpu.VMEM((ROWS, WIDTH), BF16),
            pltpu.VMEM((WIDTH + 16, WIDTH), F32),
            pltpu.VMEM((3, WIDTH + 16, TILE), F32),
            pltpu.VMEM((WIDTH + 16, 6 * TILE), BF16),
            pltpu.VMEM((WIDTH, 6 * TILE), BF16),
            pltpu.VMEM((2 * TILE, 6 * TILE), BF16),
            pltpu.VMEM((4, TILE, TILE), F32),
            pltpu.VMEM((TILE, TILE), F32),
            pltpu.SemaphoreType.DMA,
        ],
        name="solve",
    )(core, count, pattern, rows, mine, other, diag, weights, resid)


def exchange(x, axes):
    return lax.all_to_all(x, axes, split_axis=0, concat_axis=0, tiled=True)


def reduce_all(keep, give):
    swap = [(0, 1), (1, 0)]
    half = keep + lax.ppermute(give, "core", swap)
    pieces = exchange(half.reshape(32, 17, TILE), ("y", "x"))
    piece = jnp.sum(pieces, axis=0)
    layers = exchange(jnp.broadcast_to(piece[None], (8, 17, TILE)), "z")
    piece = jnp.sum(layers, axis=0)
    half = exchange(jnp.broadcast_to(piece[None], (32, 17, TILE)), ("y", "x")).reshape(HALF, TILE)
    return half, lax.ppermute(half, "core", swap)


def on_device(link_rows, barrier_weights, row_residual, tile_pattern, block_rows, link_diag):
    weights = barrier_weights.reshape(TILES, TILE)
    resid = row_residual.reshape(TILES, TILE)
    core = lax.axis_index("core").astype(jnp.int32).reshape(1)
    pattern = tile_pattern.T
    mine, other = reduce_all(*assemble(core, block_rows, pattern, link_rows, weights, resid))
    mine = pltpu.with_memory_space_constraint(mine, pltpu.VMEM)
    other = pltpu.with_memory_space_constraint(other, pltpu.VMEM)
    row_step, step = solve(core, block_rows, pattern, link_rows, mine, other, link_diag.reshape(4, TILE), weights, resid)
    return row_step.reshape(ROWS), step.reshape(WIDTH)


def solution(mesh):
    fine = Mesh(mesh.devices.reshape(8, 2, 8, 4), NAMES)
    return jax.shard_map(
        on_device,
        mesh=fine,
        in_specs=(P(NAMES, None), P(NAMES), P(NAMES), P(NAMES, None), P(NAMES), P()),
        out_specs=(P(NAMES), P()),
        check_vma=False,
    )
```

```python
import functools

import jax
import jax.numpy as jnp
from jax import lax
from jax.experimental import pallas as pl
from jax.experimental.pallas import tpu as pltpu
from jax.sharding import Mesh, PartitionSpec as P

TILE = 128
WIDTH = 512
ROWS = 2048
TILES = ROWS // TILE
CHUNKS = 4
F32 = jnp.float32
BF16 = jnp.bfloat16
HIGH = lax.Precision.HIGHEST
HALF = 544
NAMES = ("z", "core", "y", "x")


def iota(shape, axis):
    return lax.broadcasted_iota(jnp.int32, shape, axis)


def dot_nn(a, b):
    return lax.dot_general(a, b, (((1,), (0,)), ((), ())), precision=HIGH, preferred_element_type=F32)


def dot_nt(a, b):
    return lax.dot_general(a, b, (((1,), (1,)), ((), ())), precision=HIGH, preferred_element_type=F32)


def assemble_kernel(
    core_ref, count_ref, pattern_ref, rows_hbm, weights_ref, resid_ref, keep_ref, give_ref, rows, scaled, sems
):
    step = ROWS // CHUNKS
    copies = [
        pltpu.make_async_copy(rows_hbm.at[pl.ds(i * step, step)], rows.at[pl.ds(i * step, step)], sems.at[i])
        for i in range(CHUNKS)
    ]
    for copy in copies:
        copy.start()
    count = count_ref[0]
    shape = (TILES, TILE)
    live = (iota(shape, 0) * TILE + iota(shape, 1) < count).astype(F32)
    weights = weights_ref[...]
    root = jnp.sqrt(weights) * live
    weighted = (weights * resid_ref[...] * live).astype(BF16).astype(F32)
    columns = jnp.concatenate([root, weighted, jnp.zeros((TILE - 2 * TILES, TILE), F32)], axis=0).T
    gradient = [jnp.zeros((8, TILE), F32) for _ in range(4)]
    for t in range(TILES):
        if t % (TILES // CHUNKS) == 0:
            copies[t // (TILES // CHUNKS)].wait()
        root_t = jnp.broadcast_to(columns[:, t : t + 1], (TILE, TILE))
        weighted_t = jnp.broadcast_to(columns[:, TILES + t : TILES + t + 1], (TILE, TILE))
        for j in range(4):
            cover = pattern_ref[j, t].astype(F32)
            x = rows[pl.ds(t * TILE, TILE), pl.ds(j * TILE, TILE)].astype(F32) * cover
            scaled[pl.ds(t * TILE, TILE), pl.ds(j * TILE, TILE)] = (x * root_t).astype(BF16)
            gradient[j] = gradient[j] + jnp.sum((x * weighted_t).reshape(TILE // 8, 8, TILE), axis=0)
    below = iota((TILE, TILE), 0) >= iota((TILE, TILE), 1)
    same = iota((TILE, TILE), 0) == iota((TILE, TILE), 1)

    def gram(i, j):
        return lax.dot_general(
            scaled[:, pl.ds(i * 256, 256)],
            scaled[:, pl.ds(j * 256, 256)],
            (((0,), (0,)), ((), ())),
            preferred_element_type=F32,
        )

    def finish(out_ref, block, corner, pieces, first):
        a, b = block[:TILE, :TILE], block[TILE:, TILE:]
        out_ref[pl.ds(0, TILE), :] = jnp.where(below, a, b)
        out_ref[pl.ds(TILE, TILE), :] = corner
        for i, piece in enumerate(pieces):
            out_ref[pl.ds((2 + i) * TILE, TILE), :] = piece
        diagonal = jnp.sum(jnp.where(same, b, 0.0), axis=0, keepdims=True)
        parts = [jnp.sum(gradient[first], axis=0, keepdims=True), jnp.sum(gradient[first + 1], axis=0, keepdims=True), diagonal]
        out_ref[pl.ds(4 * TILE, 8), :] = jnp.concatenate(parts + [jnp.zeros((5, TILE), F32)], axis=0)
        out_ref[pl.ds(4 * TILE + 8, 24), :] = jnp.zeros((24, TILE), F32)

    top, low, cross = gram(0, 0), gram(1, 1), gram(1, 0)

    def both(first_ref, second_ref):
        finish(first_ref, top, top[TILE:, :TILE], (cross[:TILE, :TILE], cross[TILE:, :TILE]), 0)
        finish(second_ref, low, low[TILE:, :TILE], (cross[:TILE, TILE:], cross[TILE:, TILE:]), 2)

    @pl.when(core_ref[0] == 0)
    def _():
        both(keep_ref, give_ref)

    @pl.when(core_ref[0] != 0)
    def _():
        both(give_ref, keep_ref)


def assemble(core, count, pattern, rows, weights, resid):
    vmem = pl.BlockSpec(memory_space=pltpu.VMEM)
    smem = pl.BlockSpec(memory_space=pltpu.SMEM)
    half = pltpu.VMEM((HALF, TILE), F32)
    return pl.pallas_call(
        assemble_kernel,
        out_shape=(half, half),
        in_specs=[smem, smem, smem, pl.BlockSpec(memory_space=pl.ANY), vmem, vmem],
        out_specs=(vmem, vmem),
        scratch_shapes=[
            pltpu.VMEM((ROWS, WIDTH), BF16),
            pltpu.VMEM((ROWS, WIDTH), BF16),
            pltpu.SemaphoreType.DMA((CHUNKS,)),
        ],
        name="assemble",
    )(core, count, pattern, rows, weights, resid)


def wide(v):
    return jnp.broadcast_to(v, (8, TILE))


def spread_lane(v, lane):
    return jnp.take_along_axis(v, jnp.full((8, TILE), lane, jnp.int32), axis=1)


def eliminate(rows, first, once, tasks):
    lane, sub = iota((8, TILE), 1), iota((8, TILE), 0)
    groups = [rows[8 * k : 8 * k + 8] for k in range(8)]
    sides = [(lane - first - 8 * k == sub).astype(F32) for k in range(8)]
    lower, scaled = [], []
    def step(k, groups, sides):
        groups, sides, start = list(groups), list(sides), first + 8 * k
        cols = [spread_lane(groups[0], start + j) for j in range(8)]
        panel, side = groups[0], sides[0]
        for j in range(0, 8, 2):
            one, two = cols[j], cols[j + 1]
            a, b, c = wide(one[j : j + 1, :]), wide(two[j : j + 1, :]), wide(two[j + 1 : j + 2, :])
            inverse = 1.0 / (a * c - b * b)
            upper, lower_row = sub == j, sub == j + 1
            both = upper | lower_row
            by_first = jnp.where(upper, -c, jnp.where(lower_row, b, one * c - two * b)) * inverse
            by_second = jnp.where(upper, b, jnp.where(lower_row, -a, two * a - one * b)) * inverse

            def pivot(v):
                x, y = wide(v[j : j + 1, :]), wide(v[j + 1 : j + 2, :])
                return jnp.where(both, 0.0, v) - (by_first * x + by_second * y)

            for i in range(j + 2, 8):
                cols[i] = pivot(cols[i])
            panel, side = pivot(panel), pivot(side)
        spread = [wide(panel[j : j + 1, :]) for j in range(8)]
        spread_side = [wide(side[j : j + 1, :]) for j in range(8)]
        for i in range(1, len(groups)):
            lead = [spread_lane(groups[i], start + j) for j in range(8)]
            groups[i] = groups[i] - add_up([lead[j] * spread[j] for j in range(8)])
            sides[i] = sides[i] - add_up([lead[j] * spread_side[j] for j in range(8)])
        return groups[1:], sides[1:], side

    for k in range(0, 8, 2):
        todo = tasks.pop(0) if tasks and k >= tasks[0][0] else None
        more = tasks.pop(0) if tasks and k >= tasks[0][0] else None

        def body(_, carry):
            for task in (todo, more):
                if task:
                    task[1]()
            rest, others, one = step(k, carry[: 8 - k], carry[8 - k :])
            after = others[0]
            rest, others, two = step(k + 1, rest, others)
            return (*rest, after, after, *others, one, two)

        lower.append(sides[0])
        carry = lax.fori_loop(0, once, body, (*groups, *sides))
        lower.append(carry[6 - k])
        groups, sides = list(carry[: 6 - k]), list(carry[8 - k : 14 - 2 * k])
        scaled += carry[14 - 2 * k :]
    return jnp.concatenate(lower, axis=0), jnp.concatenate(scaled, axis=0)


def add_up(terms):
    while len(terms) > 1:
        terms = [terms[i] + terms[i + 1] for i in range(0, len(terms), 2)]
    return terms[0]


def thirds(x):
    high = x.astype(BF16)
    rest = x - high.astype(F32)
    middle = rest.astype(BF16)
    return high, middle, (rest - middle.astype(F32)).astype(BF16)


def as_left(x):
    h, m, l = thirds(x)
    return jnp.concatenate([h, m, h, m, h, l], axis=1)


def as_right(x, axis=1):
    h, m, l = thirds(x)
    return jnp.concatenate([h, h, m, m, l, h], axis=axis)


def times(left, right, dim=1):
    return lax.dot_general(left, right, (((1,), (dim,)), ((), ())), preferred_element_type=F32)


def factor(block, once, cross, tasks):
    half = TILE // 2
    zeros = jnp.zeros((half, TILE), F32)
    low = block[half:]
    lower, scaled = eliminate(block[:half], 0, once, tasks)
    pair = times(as_left(low), as_right(jnp.concatenate([lower, zeros, scaled, zeros], axis=0)))
    left = as_left(pair[:, :TILE])
    low = low - times(left, as_right(jnp.concatenate([zeros, pair[:, TILE:]], axis=0)))
    cross[pl.ds(half, half), :] = times(left, as_right(jnp.concatenate([scaled, zeros], axis=0), 0), 0)
    both = jnp.concatenate(eliminate(low, half, once, tasks), axis=0)
    both = both - times(as_left(both), as_right(cross[...], 0), 0)
    return jnp.concatenate([lower, both[:half]], axis=0), jnp.concatenate([scaled, both[half:]], axis=0)


def solve_kernel(
    core_ref, count_ref, pattern_ref, rows_hbm, mine_ref, other_ref, diag_ref, weights_ref, resid_ref,
    row_step_ref, step_ref, rows, matrix, lefts, left_parts, right_parts, both_parts, scales, cross, sem,
):
    copy = pltpu.make_async_copy(rows_hbm, rows, sem)
    copy.start()
    below = iota((TILE, TILE), 0) >= iota((TILE, TILE), 1)
    same = iota((TILE, TILE), 0) == iota((TILE, TILE), 1)
    link = diag_ref[...]
    core = core_ref[0]

    def tile(i, j):
        return pl.ds(i * TILE, TILE), pl.ds(j * TILE, TILE)

    gradient = []
    for h in range(2):

        def part(start, size):
            return jnp.where(core == h, mine_ref[pl.ds(start, size), :], other_ref[pl.ds(start, size), :])

        folded = part(0, TILE)
        turned = folded.T
        extras = part(4 * TILE, 8)
        gradient += [extras[0:1], extras[1:2]]
        i = 2 * h
        matrix[tile(i, i)] = jnp.where(below, folded, turned) + jnp.where(same, link[i : i + 1, :], 0.0)
        matrix[tile(i + 1, i + 1)] = jnp.where(same, extras[2:3] + link[i + 1 : i + 2, :], jnp.where(below, turned, folded))
        matrix[tile(i + 1, i)] = part(TILE, TILE)
        matrix[tile(2, h)] = part(2 * TILE, TILE)
        matrix[tile(3, h)] = part(3 * TILE, TILE)
    once = jnp.minimum(count_ref[0], 1)
    cross[...] = jnp.zeros((TILE, TILE), F32)
    matrix[pl.ds(WIDTH, 16), :] = jnp.broadcast_to(jnp.concatenate(gradient, axis=1), (16, WIDTH))

    def span(i):
        return pl.ds(i * TILE, TILE if i < 3 else TILE + 16)

    def project(i, q, both):
        pair = times(as_left(matrix[span(i), pl.ds(q * TILE, TILE)]), both)
        lefts[q, span(i), :] = pair[:, :TILE]
        left_parts[span(i), :] = as_left(pair[:, :TILE])
        right_parts[pl.ds(i * TILE, TILE), :] = as_right(pair[:TILE, TILE:])

    def update(i, j, count):
        columns = pl.ds(j * TILE, count * TILE)
        matrix[span(i), columns] -= times(left_parts[span(i), :], right_parts[columns, :])

    tasks = []
    for q in range(4):
        lower, scaled = factor(matrix[tile(q, q)], once, cross, tasks)
        assert not tasks
        scales[q] = scaled
        both_parts[...] = as_right(jnp.concatenate([lower, scaled], axis=0))
        if q == 3:
            break
        project(q + 1, q, both_parts[...])
        update(q + 1, q + 1, 1)
        for i in range(q + 2, 4):
            tasks.append((1, functools.partial(lambda i, q: project(i, q, both_parts[...]), i, q)))
        for i in range(q + 2, 4):
            tasks.append((1, functools.partial(update, i, q + 1, 2)))
            if i == q + 3:
                tasks.append((1, functools.partial(update, i, i, 1)))
    last = times(as_left(matrix[pl.ds(WIDTH, 16), pl.ds(3 * TILE, TILE)]), both_parts[pl.ds(0, TILE), :])
    steps = [None] * 4
    for q in reversed(range(4)):
        value = last[:1] if q == 3 else lefts[q, pl.ds(WIDTH, 8), :][:1]
        for i in range(q + 1, 4):
            value = value - dot_nn(steps[i], lefts[q, pl.ds(i * TILE, TILE), :])
        steps[q] = dot_nn(value, scales[q])
    step_ref[...] = jnp.concatenate(steps, axis=0)
    copy.wait()
    shape = (TILES, TILE)
    left = []
    for j in range(4):
        present = jnp.zeros(shape, F32)
        for t in range(TILES):
            present = jnp.where(iota(shape, 0) == t, pattern_ref[j, t].astype(F32), present)
        left.append(jnp.broadcast_to(steps[j], shape) * present)
    left = jnp.concatenate(left, axis=1).astype(BF16)
    moved = jnp.zeros(shape, F32)
    for t in range(TILES):
        part = lax.dot_general(
            left, rows[pl.ds(t * TILE, TILE), :], (((1,), (1,)), ((), ())), preferred_element_type=F32
        )
        moved = jnp.where(iota(shape, 0) == t, part, moved)
    live = (iota(shape, 0) * TILE + iota(shape, 1) < count_ref[0]).astype(F32)
    row_step_ref[...] = live * weights_ref[...] * (moved - resid_ref[...])


def solve(core, count, pattern, rows, mine, other, diag, weights, resid):
    vmem = pl.BlockSpec(memory_space=pltpu.VMEM)
    smem = pl.BlockSpec(memory_space=pltpu.SMEM)
    return pl.pallas_call(
        solve_kernel,
        out_shape=(jax.ShapeDtypeStruct((TILES, TILE), F32), jax.ShapeDtypeStruct((4, TILE), F32)),
        in_specs=[smem, smem, smem, pl.BlockSpec(memory_space=pl.ANY)] + [vmem] * 5,
        out_specs=(vmem, vmem),
        scratch_shapes=[
            pltpu.VMEM((ROWS, WIDTH), BF16),
            pltpu.VMEM((WIDTH + 16, WIDTH), F32),
            pltpu.VMEM((3, WIDTH + 16, TILE), F32),
            pltpu.VMEM((WIDTH + 16, 6 * TILE), BF16),
            pltpu.VMEM((WIDTH, 6 * TILE), BF16),
            pltpu.VMEM((2 * TILE, 6 * TILE), BF16),
            pltpu.VMEM((4, TILE, TILE), F32),
            pltpu.VMEM((TILE, TILE), F32),
            pltpu.SemaphoreType.DMA,
        ],
        name="solve",
    )(core, count, pattern, rows, mine, other, diag, weights, resid)


def exchange(x, axes):
    return lax.all_to_all(x, axes, split_axis=0, concat_axis=0, tiled=True)


def reduce_all(keep, give):
    swap = [(0, 1), (1, 0)]
    half = keep + lax.ppermute(give, "core", swap)
    pieces = exchange(half.reshape(32, 17, TILE), ("y", "x"))
    piece = jnp.sum(pieces, axis=0)
    layers = exchange(jnp.broadcast_to(piece[None], (8, 17, TILE)), "z")
    piece = jnp.sum(layers, axis=0)
    half = exchange(jnp.broadcast_to(piece[None], (32, 17, TILE)), ("y", "x")).reshape(HALF, TILE)
    return half, lax.ppermute(half, "core", swap)


def on_device(link_rows, barrier_weights, row_residual, tile_pattern, block_rows, link_diag):
    weights = barrier_weights.reshape(TILES, TILE)
    resid = row_residual.reshape(TILES, TILE)
    core = lax.axis_index("core").astype(jnp.int32).reshape(1)
    pattern = tile_pattern.T
    mine, other = reduce_all(*assemble(core, block_rows, pattern, link_rows, weights, resid))
    mine = pltpu.with_memory_space_constraint(mine, pltpu.VMEM)
    other = pltpu.with_memory_space_constraint(other, pltpu.VMEM)
    row_step, step = solve(core, block_rows, pattern, link_rows, mine, other, link_diag.reshape(4, TILE), weights, resid)
    return row_step.reshape(ROWS), step.reshape(WIDTH)


def solution(mesh):
    fine = Mesh(mesh.devices.reshape(8, 2, 8, 4), NAMES)
    return jax.shard_map(
        on_device,
        mesh=fine,
        in_specs=(P(NAMES, None), P(NAMES), P(NAMES), P(NAMES, None), P(NAMES), P()),
        out_specs=(P(NAMES), P()),
        check_vma=False,
    )
```
